32 devices in a mesh: dp: 8 (over z, y), ctx: 4 (over x, core).
Axes of the slice: x: 2, y: 2, z: 4, core: 2. Of those that a mesh axis runs over, the one named last changes fastest.
Arguments:
- student_queries: bfloat16 [8, 512, 2048], P('dp', 'ctx'), may hold values from -8 to 8
- student_keys: bfloat16 [8, 512, 512], P('dp', 'ctx'), may hold values from -8 to 8
- teacher_maps: bfloat16 [8, 16, 512, 512], P('dp', 'ctx'), may hold values from 0.049804688 to 5
- lengths: int32 [8], P('dp'), may hold values from 256 to 512
- hidden_in: bfloat16 [8, 512, 4096], P('dp', 'ctx'), may hold values from -6 to 6
- adapter_in: bfloat16 [8, 512, 128], P('dp', 'ctx'), may hold values from -6 to 6
- adapter_up: bfloat16 [2560, 64], replicated, may hold values from -0.75 to 0.75
Outputs:
- grad_down: float32 [4096, 128], P(('dp', 'ctx'))
- grad_up: float32 [2560, 64], P(('dp', 'ctx'))
The draws below stay inside these ranges and needn't reach their ends.
All inputs are finite; a program needn't handle non-finite values.
Results may differ from the reference program's by a relative error of at most 0.0049.
Values may be sent and summed in bfloat16 or wider, within the bound.
No kernel may reach another device: no remote copies, remote signals or barrier semaphores. Data moves between devices by JAX's collectives and lax.ppermute only.
A program may use at most 64 MiB of HBM per device.

```python
import math
import jax
import jax.numpy as jnp
from jax import lax

D = 4096
DH = 128
H = 16
KV = 4
R = 64
SEQ = 512
BATCH = 8


def draw_student_queries(key, part):
    own_key = jax.random.fold_in(key, 11)
    base_noise = jax.random.normal(own_key, (BATCH, SEQ, H, DH), jnp.float32)
    return jnp.clip(base_noise, -8.0, 8.0).reshape(BATCH, SEQ, H * DH).astype(jnp.bfloat16)


def draw_student_keys(key, part):
    own_key = jax.random.fold_in(key, 23)
    base_noise = jax.random.normal(own_key, (BATCH, SEQ, KV, DH), jnp.float32)
    return jnp.clip(base_noise, -8.0, 8.0).reshape(BATCH, SEQ, KV * DH).astype(jnp.bfloat16)


def touch_ends(values, stream_key, least, top_value):
    longest = values.shape.index(max(values.shape))
    spots = []
    for shift in (0, 1):
        where = [jax.random.randint(jax.random.fold_in(stream_key, axis), (), 0, length) for axis, length in enumerate(values.shape)]
        where[longest] = (where[longest] + shift) % values.shape[longest]
        spots.append(tuple(where))
    return values.at[spots[0]].set(least).at[spots[1]].set(top_value)


def spiked(values, rng, source, target, blocks, factor):
    owner, partner = [(jnp.arange(values.shape[position]) // (values.shape[position] // blocks)).reshape([-1 if axis == position else 1 for axis in range(values.ndim)]) for position in (source, target)]
    chosen = jax.random.permutation(rng, blocks)[partner]
    strong = (owner == chosen) | (owner == (partner + blocks // 2) % blocks)
    return jnp.where(strong, factor * values, values)


def block_levels(key, shape, pieces, smallest, largest):
    def one(axis_at, blocks):
        steps = jax.random.uniform(jax.random.fold_in(jax.random.fold_in(key, 6), axis_at), (blocks,), jnp.float32, smallest / len(pieces), largest / len(pieces))
        return jnp.repeat(jnp.exp(steps), shape[axis_at] // blocks).reshape((-1,) + (1,) * (len(shape) - axis_at - 1))

    factor_of = one(*pieces[0])
    for cut in pieces[1:]:
        factor_of = factor_of * one(*cut)
    return factor_of


def bell_draw(key, dims, spread, limit, pieces=(), kind=jnp.bfloat16):
    values = jax.random.normal(key, dims, jnp.float32) * spread
    if len(pieces) > 0:
        values = block_levels(key, dims, pieces, -0.22, 0.18) * values
    return jnp.clip(values, min=-limit, max=limit).astype(kind)


def noise_with(stream_key, shape, deviation, bound, pieces, heavy, held_as=jnp.bfloat16):
    values = deviation * jax.random.normal(stream_key, shape, jnp.float32)
    if pieces:
        values = values * block_levels(stream_key, shape, pieces, -0.22, 0.18)
    return jnp.clip(spiked(values, jax.random.fold_in(stream_key, 3), *heavy), -bound, bound).astype(held_as)


def setup_inputs(seed: int = 0) -> dict:
    streams_of = jax.random.split(jax.random.key(seed), 8)
    return {
        "student_queries": draw_student_queries(jax.random.fold_in(streams_of[7], 71), 0),
        "student_keys": draw_student_keys(jax.random.fold_in(streams_of[7], 71), 0),
        "teacher_maps": jnp.clip(jnp.exp(math.log(5.0) - 4.609084 * jax.random.uniform(streams_of[2], (BATCH, H, SEQ, SEQ), jnp.float32) ** block_levels(streams_of[2], (BATCH, H, SEQ, SEQ), ((0, 8), (1, 4)), -0.2, 0.2)), 0.049804688, 5.0).astype(jnp.bfloat16),
        "lengths": touch_ends(jax.random.randint(streams_of[3], (BATCH,), SEQ // 2, SEQ + 1), jax.random.fold_in(streams_of[3], 1), SEQ // 2, SEQ).astype(jnp.int32),
        "hidden_in": noise_with(streams_of[4], (BATCH, SEQ, D), 1.0, 6.0, ((0, 8), (1, 4)), (1, 2, 4, 2.0)),
        "adapter_in": bell_draw(streams_of[5], (BATCH, SEQ, 2 * R), 1.0, 6.0, ((0, 8), (1, 4))),
        "adapter_up": bell_draw(streams_of[6], ((H + KV) * DH, R), R ** -0.5, 0.75),
    }


def head_backward(queries, keys_one, teacher, length):
    block_rows = min(512, SEQ)
    score_scale = 1.0 / math.sqrt(DH)
    key_pos = jnp.arange(SEQ, dtype=jnp.int32)

    def one_block(dk_accum, block_idx):
        row_start = block_idx * block_rows
        query_blk = lax.dynamic_slice_in_dim(queries, row_start, block_rows, 0)
        teach_blk = lax.dynamic_slice_in_dim(teacher, row_start, block_rows, 0).astype(jnp.float32)
        row_pos = row_start + jnp.arange(block_rows, dtype=jnp.int32)
        visible = (key_pos[None, :] <= row_pos[:, None]) & (key_pos[None, :] < length)
        scores = jnp.dot(query_blk, keys_one.T, preferred_element_type=jnp.float32) * score_scale
        scores = jnp.where(visible, scores, -jnp.inf)
        row_peak = lax.optimization_barrier(jnp.max(scores, axis=1, keepdims=True))
        exp_scores = jnp.exp(scores - row_peak)
        student = exp_scores / lax.optimization_barrier(jnp.sum(exp_scores, axis=1, keepdims=True))
        masked_teacher = jnp.where(visible, teach_blk, 0.0)
        target = masked_teacher / lax.optimization_barrier(jnp.sum(masked_teacher, axis=1, keepdims=True))
        weight_row = jnp.where(row_pos < length, 1.0 / H, 0.0)
        grad_scores = ((student - target) * weight_row[:, None]).astype(jnp.bfloat16)
        dq_blk = (jnp.dot(grad_scores, keys_one, preferred_element_type=jnp.float32) * score_scale).astype(jnp.bfloat16)
        dk_accum = dk_accum + jnp.dot(grad_scores.T, query_blk, preferred_element_type=jnp.float32)
        return (dk_accum, dq_blk)
    dk_total, dq_blocks = lax.scan(one_block, jnp.zeros((SEQ, DH), jnp.float32), jnp.arange(SEQ // block_rows, dtype=jnp.int32))
    return (dq_blocks.reshape(SEQ, DH), (dk_total * score_scale).astype(jnp.bfloat16))

def reference(student_queries, student_keys, teacher_maps, lengths, hidden_in, adapter_in, adapter_up):
    group_size = H // KV

    def one_sequence(seq_items):
        queries, keys_seq, teacher, length, hidden, adapter_loc = seq_items
        q_heads = queries.reshape(SEQ, H, DH).transpose(1, 0, 2)
        k_heads = jnp.repeat(keys_seq.reshape(SEQ, KV, DH).transpose(1, 0, 2), group_size, axis=0)

        def per_head(head_items):
            return head_backward(head_items[0], head_items[1], head_items[2], length)
        dq_heads, dk_heads = lax.map(per_head, (q_heads, k_heads, teacher))
        grad_q = dq_heads.transpose(1, 0, 2).reshape(SEQ, H * DH)
        grad_k = lax.optimization_barrier(jnp.sum(dk_heads.astype(jnp.float32).reshape(KV, group_size, SEQ, DH), axis=1))
        grad_k = grad_k.astype(jnp.bfloat16).transpose(1, 0, 2).reshape(SEQ, KV * DH)
        low_q = jnp.dot(grad_q, adapter_up[:H * DH], preferred_element_type=jnp.float32)
        low_k = jnp.dot(grad_k, adapter_up[H * DH:], preferred_element_type=jnp.float32)
        lowered = jnp.concatenate([low_q, low_k], axis=1).astype(jnp.bfloat16)
        down_grad = jnp.dot(hidden.T, lowered, preferred_element_type=jnp.float32)
        up_grad = jnp.concatenate([jnp.dot(grad_q.T, adapter_loc[:, :R], preferred_element_type=jnp.float32), jnp.dot(grad_k.T, adapter_loc[:, R:], preferred_element_type=jnp.float32)], axis=0)
        return (down_grad, up_grad)
    down_grads, up_grads = lax.map(one_sequence, (student_queries, student_keys, teacher_maps, lengths, hidden_in, adapter_in))
    return (lax.optimization_barrier(jnp.sum(down_grads, axis=0)), lax.optimization_barrier(jnp.sum(up_grads, axis=0)))
```

```python
import functools
import math

import jax
import jax.numpy as jnp
import numpy as np
from jax import lax
from jax.experimental import pallas as pl
from jax.experimental.pallas import tpu as pltpu
from jax.sharding import PartitionSpec as P

NT = (((1,), (1,)), ((), ()))
TN = (((0,), (0,)), ((), ()))


def dot32(a, b, dims=(((1,), (0,)), ((), ()))):
    return lax.dot_general(a, b, dims, preferred_element_type=jnp.float32)


def owner_tables(C, Dp, W, Wk, DH, q_width, group_cols, rows_total, lane_block):
    rows_each = rows_total // (C * Dp)
    local = []
    for c in range(C):
        k_start = q_width + (c * W // group_cols) * DH
        local.append(np.concatenate([c * W + np.arange(W), k_start + np.arange(Wk)]))
    owner = [rows // rows_each for rows in local]
    most = max(int(np.sum(o % C == dst)) for o in owner for dst in range(C))
    slot = -(-most // 128) * 128
    pack = np.full((C, C, slot), -1, np.int32)
    land = np.full((C, C, slot), -1, np.int32)
    rows_of = {}
    for c in range(C):
        for dst in range(C):
            mine = np.nonzero(owner[c] % C == dst)[0]
            rows_of[c, dst] = mine
    for me in range(C):
        for s in range(C):
            mine = rows_of[me, me ^ s]
            pack[me, s, : len(mine)] = mine
            src = me ^ s
            sent = local[src][rows_of[src, me]]
            blk = sent // rows_each
            land[me, s, : len(sent)] = blk // C * lane_block + sent % rows_each
    return pack, land, slot, rows_each


def attend_kernel(C, tok, hq, kh, DH, H, R, scalars, *refs):
    q_in, k_in, a_in = refs[:C], refs[C : 2 * C], refs[2 * C : 3 * C]
    teacher, up_q, up_k, pack = refs[3 * C : 3 * C + 4]
    low_out, grad_out = refs[3 * C + 4 : 3 * C + 6]
    q_buf, k_buf, a_buf, dq_buf, dk_buf = refs[3 * C + 6 :]
    me, length = scalars[0], scalars[1]
    per_key = hq // kh
    scale = 1.0 / math.sqrt(DH)
    exp_scale = scale * math.log2(math.e)
    for s in range(C):
        row = pl.multiple_of(jnp.bitwise_xor(me, s) * tok, tok)
        for h in range(hq):
            q_buf[h, pl.ds(row, tok), :] = q_in[s][:, h * DH : (h + 1) * DH]
        k_buf[pl.ds(row, tok), :] = k_in[s][...]
        a_buf[pl.ds(row, tok), :] = a_in[s][...]
    dk_buf[...] = jnp.zeros_like(dk_buf)
    row_in = lax.broadcasted_iota(jnp.int32, (tok, 1), 0)
    col_in = lax.broadcasted_iota(jnp.int32, (tok, tok), 1)
    for p in range(C):
        start, ext = p * tok, (p + 1) * tok
        row_pos = row_in + start
        visible = (col_in + start) <= jnp.minimum(row_pos, length - 1)
        weight = jnp.where(row_pos < length, 1.0 / H, 0.0)
        for g in range(kh):
            keys = k_buf[:ext, g * DH : (g + 1) * DH]
            heads = range(g * per_key, (g + 1) * per_key)
            q_all = q_buf[g * per_key : (g + 1) * per_key, start:ext, :].reshape(per_key * tok, DH)
            scores = dot32(q_all, keys, NT)
            grads = []
            for n, h in enumerate(heads):
                sc = scores[n * tok : (n + 1) * tok]
                diag = jnp.where(visible, sc[:, start:], -1e30)
                sc = diag if p == 0 else jnp.concatenate([sc[:, :start], diag], axis=1)
                te_d = jnp.where(visible, teacher[h, start:ext, start:ext].astype(jnp.float32), 0.0)
                te = te_d if p == 0 else jnp.concatenate(
                    [teacher[h, start:ext, :start].astype(jnp.float32), te_d], axis=1
                )
                ex = jnp.exp2((sc - jnp.max(sc, axis=1, keepdims=True)) * exp_scale)
                w_s = weight / jnp.sum(ex, axis=1, keepdims=True)
                w_t = weight / jnp.sum(te, axis=1, keepdims=True)
                grads.append((ex * w_s - te * w_t).astype(jnp.bfloat16))
            grad = grads[0] if per_key == 1 else jnp.concatenate(grads, axis=0)
            dq = (dot32(grad, keys) * scale).astype(jnp.bfloat16)
            for n, h in enumerate(heads):
                dq_buf[start:ext, h * DH : (h + 1) * DH] = dq[n * tok : (n + 1) * tok]
            dk_buf[g * DH : (g + 1) * DH, :ext] += dot32(q_all, grad, TN)
    dq = dq_buf[...]
    dk = (dk_buf[...] * scale).astype(jnp.bfloat16)
    low_out[:R, :] = dot32(up_q[...], dq, NT).astype(low_out.dtype)
    low_out[R:, :] = dot32(up_k[...], dk).astype(low_out.dtype)
    a_q, a_k = a_buf[:, :R], a_buf[:, R:]
    grad_up = jnp.concatenate(
        [dot32(a_q, dq, TN).astype(jnp.bfloat16), dot32(a_k.T, dk, NT).astype(jnp.bfloat16)], axis=1
    )
    pick = lax.broadcasted_iota(jnp.int32, (grad_up.shape[1], pack.shape[1]), 0) == pack[...]
    pick = jnp.where(pick, 1.0, 0.0).astype(jnp.bfloat16)
    grad_out[...] = dot32(grad_up, pick).astype(grad_out.dtype)


def down_kernel(C, Dp, tok, R, rblk, scalars, *refs):
    low_a, low_b = refs[:2]
    hid = refs[2 : 2 + C]
    got = refs[2 + C : 2 + 2 * C]
    land, out = refs[2 + 2 * C :]
    me = scalars[0]
    acc = None
    low = (low_a[...].astype(jnp.float32) + low_b[...].astype(jnp.float32)).astype(jnp.bfloat16)
    blocks = [low[:, p * tok : (p + 1) * tok] for p in range(C)]
    for s in range(C):
        pos = jnp.bitwise_xor(me, s)
        part = blocks[0]
        for p in range(1, C):
            part = jnp.where(pos == p, blocks[p], part)
        term = dot32(part, hid[s][...])
        acc = term if acc is None else acc + term
    rows = jnp.concatenate([g[...] for g in got], axis=1)
    place = lax.broadcasted_iota(jnp.int32, (Dp * rblk, rows.shape[1]), 0) == land[...]
    place = jnp.where(place, 1.0, 0.0).astype(jnp.bfloat16)
    ups = dot32(rows, place, NT)
    for d in range(Dp):
        out[d, : 2 * R, :] = acc[:, d * rblk : (d + 1) * rblk].astype(out.dtype)
        out[d, 2 * R :, :] = ups[:, d * rblk : (d + 1) * rblk].astype(out.dtype)


def final_kernel(R, rows_each, got, down, up):
    total = jnp.sum(got[...].astype(jnp.float32), axis=0)
    down[...] = total[: 2 * R].T
    up[...] = total[2 * R :, :rows_each]


def solution(mesh):
    C, Dp = mesh.shape["ctx"], mesh.shape["dp"]

    def swap(x, s):
        return lax.ppermute(x, "ctx", [(i, i ^ s) for i in range(C)])

    def body(queries, keys, teacher, lengths, hidden, adapter, adapter_up):
        tok = queries.shape[1]
        hq = teacher.shape[1]
        S = teacher.shape[2]
        H = hq * C
        DH = queries.shape[2] // H
        KV = keys.shape[2] // DH
        R = adapter.shape[2] // 2
        D = hidden.shape[2]
        q_width = H * DH
        rows_total = adapter_up.shape[0]
        kh = max(1, KV // C)
        W, Wk = hq * DH, kh * DH
        rblk = D // (C * Dp)
        group_cols = (H // KV) * DH
        me = lax.axis_index("ctx")
        queries, keys, hidden, adapter = queries[0], keys[0], hidden[0], adapter[0]

        def key_col(dst):
            return (dst * W // group_cols) * DH

        q_blk, k_blk, a_blk, h_blk = [], [], [], []
        for s in range(C):
            dst = me ^ s
            q_blk.append(lax.dynamic_slice_in_dim(queries, dst * W, W, 1))
            k_blk.append(lax.dynamic_slice_in_dim(keys, key_col(dst), Wk, 1))
            if rblk % 128 == 0:
                cols = [lax.dynamic_slice_in_dim(hidden, (d * C + dst) * rblk, rblk, 1) for d in range(Dp)]
                h_blk.append(jnp.concatenate(cols, axis=1))
            else:
                cols = lax.dynamic_index_in_dim(hidden.reshape(tok, Dp, C, rblk), dst, 2, keepdims=False)
                h_blk.append(cols.reshape(tok, Dp * rblk))
        for s in range(1, C):
            q_blk[s] = swap(q_blk[s], s)
            k_blk[s] = swap(k_blk[s], s)
        a_blk = [adapter] + [swap(adapter, s) for s in range(1, C)]
        for s in range(1, C):
            h_blk[s] = swap(h_blk[s], s)

        pack, land, slot, rows_each = owner_tables(C, Dp, W, Wk, DH, q_width, group_cols, rows_total, rblk)
        pack_me = lax.dynamic_index_in_dim(jnp.asarray(pack.reshape(C, 1, C * slot)), me, 0, keepdims=False)
        land_me = lax.dynamic_index_in_dim(jnp.asarray(land.reshape(C, 1, C * slot)), me, 0, keepdims=False)
        up_t = adapter_up.T
        up_q = lax.dynamic_slice_in_dim(up_t, me * W, W, 1)
        up_k = lax.dynamic_slice_in_dim(up_t, q_width + key_col(me), Wk, 1)
        scalars = jnp.stack([me.astype(jnp.int32), lengths[0]])

        smem = pl.BlockSpec(memory_space=pltpu.SMEM)
        vmem = pl.BlockSpec(memory_space=pltpu.VMEM)
        bf = jnp.bfloat16
        low, packed = pl.pallas_call(
            functools.partial(attend_kernel, C, tok, hq, kh, DH, H, R),
            out_shape=(jax.ShapeDtypeStruct((2 * R, S), bf), jax.ShapeDtypeStruct((R, C * slot), bf)),
            in_specs=[smem] + [vmem] * (3 * C + 4),
            out_specs=(vmem, vmem),
            scratch_shapes=[
                pltpu.VMEM((hq, S, DH), bf),
                pltpu.VMEM((S, Wk), bf),
                pltpu.VMEM((S, 2 * R), bf),
                pltpu.VMEM((S, W), bf),
                pltpu.VMEM((Wk, S), jnp.float32),
            ],
            name="attend",
        )(scalars, *q_blk, *k_blk, *a_blk, teacher[0], up_q, up_k, pack_me)

        got = [packed[:, :slot]]
        for s in range(1, C):
            got.append(swap(packed[:, s * slot : (s + 1) * slot], s))
        bit = 1
        other = swap(low, bit)
        while bit * 2 < C:
            low = (low.astype(jnp.float32) + other.astype(jnp.float32)).astype(bf)
            bit *= 2
            other = swap(low, bit)

        msg = pl.pallas_call(
            functools.partial(down_kernel, C, Dp, tok, R, rblk),
            out_shape=jax.ShapeDtypeStruct((Dp, 3 * R, rblk), bf),
            in_specs=[smem] + [vmem] * (2 * C + 3),
            out_specs=vmem,
            name="down",
        )(scalars, low, other, *h_blk, *got, land_me)
        msg = lax.all_to_all(msg, "dp", split_axis=0, concat_axis=0, tiled=True)
        down, up = pl.pallas_call(
            functools.partial(final_kernel, R, rows_each),
            out_shape=(
                jax.ShapeDtypeStruct((rblk, 2 * R), jnp.float32),
                jax.ShapeDtypeStruct((R, rows_each), jnp.float32),
            ),
            in_specs=[vmem],
            out_specs=(vmem, vmem),
            name="final",
        )(msg)
        return down, up.T

    placed = (
        P("dp", "ctx", None),
        P("dp", "ctx", None),
        P("dp", "ctx", None, None),
        P("dp"),
        P("dp", "ctx", None),
        P("dp", "ctx", None),
        P(),
    )
    return jax.shard_map(
        body,
        mesh=mesh,
        in_specs=placed,
        out_specs=(P(("dp", "ctx"), None), P(("dp", "ctx"), None)),
        check_vma=False,
    )
```

```python
import functools
import math

import jax
import jax.numpy as jnp
import numpy as np
from jax import lax
from jax.experimental import pallas as pl
from jax.experimental.pallas import tpu as pltpu
from jax.sharding import PartitionSpec as P

NT = (((1,), (1,)), ((), ()))
TN = (((0,), (0,)), ((), ()))


def dot32(a, b, dims=(((1,), (0,)), ((), ()))):
    return lax.dot_general(a, b, dims, preferred_element_type=jnp.float32)


def owner_tables(C, Dp, W, Wk, DH, q_width, group_cols, rows_total, lane_block, lanes):
    rows_each = rows_total // (C * Dp)
    local = []
    for c in range(C):
        k_start = q_width + (c * W // group_cols) * DH
        local.append(np.concatenate([c * W + np.arange(W), k_start + np.arange(Wk)]))

    def chosen(c, core, y):
        owner = local[c] // rows_each
        return np.nonzero((owner % C % 2 == core) & (owner // C % 2 == y))[0]

    most = max(len(chosen(c, core, y)) for c in range(C) for core in (0, 1) for y in (0, 1))
    slot = -(-most // lanes) * lanes
    pack = np.full((C, 2, 4, slot), -1, np.int32)
    land = np.full((C, 2, 4, slot), -1, np.int32)
    for c in range(C):
        for y in (0, 1):
            for n in range(4):
                there, across = n % 2, n // 2
                rows = chosen(c, c % 2 ^ there, y ^ across)
                pack[c, y, n, : len(rows)] = rows
                src = c ^ there
                rows = local[src][chosen(src, c % 2, y)]
                owner = rows // rows_each
                block = (owner // C // 2) * (C // 2) + owner % C // 2
                land[c, y, n, : len(rows)] = block * lane_block + rows % rows_each
    return pack.reshape(C * 2, 4 * slot), land.reshape(C * 2, 4 * slot), slot, rows_each


def slice_kernel(plan, n_in, *refs):
    ins, (*outs, sems) = refs[:n_in], refs[n_in:]
    copies = []
    for n, (i, src, o, dst, width) in enumerate(plan(lax.axis_index("ctx"), lax.axis_index("dp"))):
        source = ins[i] if src is None else ins[i].at[..., pl.ds(src, width)]
        target = outs[o] if dst is None else outs[o].at[..., pl.ds(dst, width)]
        copies.append(pltpu.make_async_copy(source, target, sems.at[n]))
    for c in copies:
        c.start()
    for c in copies:
        c.wait()


def slices(plan, count, ins, out_shapes):
    spec = pl.BlockSpec(memory_space=pltpu.HBM)
    vmem = pl.BlockSpec(memory_space=pltpu.VMEM)
    ins = [pltpu.with_memory_space_constraint(x, pltpu.HBM) for x in ins]
    return pl.pallas_call(
        functools.partial(slice_kernel, plan, len(ins)),
        out_shape=tuple(out_shapes),
        in_specs=[spec] * len(ins),
        out_specs=tuple([vmem] * len(out_shapes)),
        scratch_shapes=[pltpu.SemaphoreType.DMA((count,))],
        compiler_params=pltpu.CompilerParams(vmem_limit_bytes=2**20),
    )(*ins)


def attend_kernel(C, tok, hq, kh, DH, H, R, lengths, *refs):
    msgs = refs[:C]
    teacher, up_q, up_k, pack = refs[C : C + 4]
    keep_out, send_out, packed_own, packed_far = refs[C + 4 : C + 8]
    q_buf, k_buf, a_buf, dq_buf, dk_buf, low_buf = refs[C + 8 :]
    me, length = lax.axis_index("ctx"), lengths[0]
    W, Wk = hq * DH, kh * DH
    per_key = hq // kh
    scale = 1.0 / math.sqrt(DH)
    exp_scale = scale * math.log2(math.e)
    for s in range(C):
        row = pl.multiple_of(jnp.bitwise_xor(me, s) * tok, tok)
        for h in range(hq):
            q_buf[h, pl.ds(row, tok), :] = msgs[s][:, h * DH : (h + 1) * DH]
        k_buf[pl.ds(row, tok), :] = msgs[s][:, W : W + Wk]
        a_buf[pl.ds(row, tok), :] = msgs[s][:, W + Wk :]
    dk_buf[...] = jnp.zeros_like(dk_buf)
    row_in = lax.broadcasted_iota(jnp.int32, (tok, 1), 0)
    col_in = lax.broadcasted_iota(jnp.int32, (tok, tok), 1)
    for p in range(C):
        start, ext = p * tok, (p + 1) * tok
        row_pos = row_in + start
        visible = (col_in + start) <= jnp.minimum(row_pos, length - 1)
        weight = jnp.where(row_pos < length, 1.0 / H, 0.0)
        for g in range(kh):
            keys = k_buf[:ext, g * DH : (g + 1) * DH]
            heads = range(g * per_key, (g + 1) * per_key)
            q_all = q_buf[g * per_key : (g + 1) * per_key, start:ext, :].reshape(per_key * tok, DH)
            scores = dot32(q_all, keys, NT)
            grads = []
            for n, h in enumerate(heads):
                sc = scores[n * tok : (n + 1) * tok]
                diag = jnp.where(visible, sc[:, start:], -1e30)
                sc = diag if p == 0 else jnp.concatenate([sc[:, :start], diag], axis=1)
                te_d = jnp.where(visible, teacher[h, start:ext, start:ext].astype(jnp.float32), 0.0)
                te = te_d if p == 0 else jnp.concatenate(
                    [teacher[h, start:ext, :start].astype(jnp.float32), te_d], axis=1
                )
                ex = jnp.exp2((sc - jnp.max(sc, axis=1, keepdims=True)) * exp_scale)
                w_s = weight / jnp.sum(ex, axis=1, keepdims=True)
                w_t = weight / jnp.sum(te, axis=1, keepdims=True)
                grads.append((ex * w_s - te * w_t).astype(jnp.bfloat16))
            grad = grads[0] if per_key == 1 else jnp.concatenate(grads, axis=0)
            dq = (dot32(grad, keys) * scale).astype(jnp.bfloat16)
            for n, h in enumerate(heads):
                dq_buf[start:ext, h * DH : (h + 1) * DH] = dq[n * tok : (n + 1) * tok]
            dk_buf[g * DH : (g + 1) * DH, :ext] += dot32(q_all, grad, TN)
    dq = dq_buf[...]
    dk = (dk_buf[...] * scale).astype(jnp.bfloat16)
    low_buf[:R, :] = dot32(up_q[...], dq, NT)
    low_buf[R:, :] = dot32(up_k[...], dk)
    far, mine = jnp.right_shift(me, 1), jnp.bitwise_and(me, 1)
    for n in range(C // 2):
        here = jnp.bitwise_xor(far, n) * 2
        keep_out[n] = low_buf[:, pl.ds(pl.multiple_of((here + mine) * tok, tok), tok)]
        send_out[n * 2 * R : (n + 1) * 2 * R, :] = low_buf[:, pl.ds(pl.multiple_of((here + 1 - mine) * tok, tok), tok)]
    a_q, a_k = a_buf[:, :R], a_buf[:, R:]
    grad_up = jnp.concatenate(
        [dot32(a_q, dq, TN).astype(jnp.bfloat16), dot32(a_k.T, dk, NT).astype(jnp.bfloat16)], axis=1
    )
    where_to = pack[pl.ds(me * 2 + jnp.bitwise_and(lax.axis_index("dp"), 1), 1), :]
    pick = lax.broadcasted_iota(jnp.int32, (grad_up.shape[1], where_to.shape[1]), 0) == where_to
    pick = jnp.where(pick, 1.0, 0.0).astype(jnp.bfloat16)
    rows = dot32(grad_up, pick)
    blks = where_to.shape[1] // 4 // tok
    for n in range(4 * blks):
        to, part = n // blks, n % blks
        dst = (packed_own, send_out, packed_far, send_out)[to]
        at = (0, C * R, 0, C * R + blks * R)[to] + part * R
        dst[at : at + R, :] = rows[:, n * tok : (n + 1) * tok].astype(dst.dtype)


def down_kernel(R, rblk, low_pair, low_other, got_own, got_pair, got_far, h0, h1, h2, h3, land, send, keep):
    lows = (low_pair[0], low_other[0], low_pair[1], low_other[1])
    acc = None
    for low, hid in zip(lows, (h0, h1, h2, h3)):
        term = dot32(low, hid[...])
        acc = term if acc is None else acc + term
    blks = got_own.shape[0] // R
    pieces = [got_own[n * R : (n + 1) * R, :] for n in range(blks)]
    pieces += [got_pair[n * R : (n + 1) * R, :].astype(jnp.bfloat16) for n in range(blks)]
    pieces += [got_far[n * R : (n + 1) * R, :] for n in range(2 * blks)]
    rows = jnp.concatenate(pieces, axis=1)
    me, me_d = lax.axis_index("ctx"), lax.axis_index("dp")
    half_c = lax.axis_size("ctx") // 2
    here = jnp.right_shift(me_d, 1) * half_c + jnp.right_shift(me, 1)
    where_to = jnp.bitwise_xor(land[pl.ds(me * 2 + jnp.bitwise_and(me_d, 1), 1), :], here * rblk)
    place = lax.broadcasted_iota(jnp.int32, (h0.shape[1], rows.shape[1]), 0) == where_to
    place = jnp.where(place, 1.0, 0.0).astype(jnp.bfloat16)
    ups = dot32(rows, place, NT)
    for e in range(h0.shape[1] // rblk):
        dst = send if e % 2 else keep
        dst[e // 2, : 2 * R, :] = acc[:, e * rblk : (e + 1) * rblk].astype(dst.dtype)
        dst[e // 2, 2 * R :, :] = ups[:, e * rblk : (e + 1) * rblk].astype(dst.dtype)


def final_kernel(R, rows_each, kept, got, down, up):
    total = kept[0] + got[0].astype(jnp.float32)
    down[...] = total[: 2 * R].T
    up[...] = total[2 * R :, :rows_each]


def solution(mesh):
    C, Dp = mesh.shape["ctx"], mesh.shape["dp"]

    def swap(x, s, axis="ctx"):
        return lax.ppermute(x, axis, [(i, i ^ s) for i in range(mesh.shape[axis])])

    def swap_diag(x):
        pairs = [(d * C + c, (d ^ 1) * C + (c ^ 1)) for d in range(Dp) for c in range(C)]
        return lax.ppermute(x, ("dp", "ctx"), pairs)

    def near(x):
        return pltpu.with_memory_space_constraint(x, pltpu.VMEM)

    def body(queries, keys, teacher, lengths, hidden, adapter, adapter_up):
        tok = queries.shape[1]
        hq = teacher.shape[1]
        S = teacher.shape[2]
        H = hq * C
        DH = queries.shape[2] // H
        KV = keys.shape[2] // DH
        R = adapter.shape[2] // 2
        D = hidden.shape[2]
        q_width = H * DH
        rows_total = adapter_up.shape[0]
        kh = max(1, KV // C)
        W, Wk = hq * DH, kh * DH
        rblk = D // (C * Dp)
        group_cols = (H // KV) * DH
        bf, f32 = jnp.bfloat16, jnp.float32

        def key_col(dst):
            return (dst * W // group_cols) * DH

        def first_plan(me, me_d):
            for s in range(C):
                dst = jnp.bitwise_xor(me, s)
                yield 0, pl.multiple_of(dst * W, 128), s, 0, W
                yield 1, pl.multiple_of(key_col(dst), 128), s, W, Wk
                yield 2, 0, s, W + Wk, 2 * R

        def second_plan(me, me_d):
            yield 0, None, 0, None, None
            yield 1, pl.multiple_of(me * W, 128), 1, 0, W
            yield 1, pl.multiple_of(q_width + key_col(me), 128), 2, 0, Wk
            yield 2, None, 3, None, None
            yield 3, None, 4, None, None
            if rblk % 128 == 0:
                for n in range(4):
                    for e in range(E):
                        yield 4, pl.multiple_of(column(me, me_d, n, e), 128), 5 + n, e * rblk, rblk

        E = C * Dp // 4

        def column(me, me_d, n, e):
            d = jnp.bitwise_xor(me_d, n // 2 + e // (C // 2) * 2)
            return (d * C + jnp.bitwise_xor(me, n % 2 + e % (C // 2) * 2)) * rblk

        pack, land, slot, rows_each = owner_tables(C, Dp, W, Wk, DH, q_width, group_cols, rows_total, rblk, tok)
        pack, land = jnp.asarray(pack), jnp.asarray(land)
        msgs = list(slices(first_plan, 3 * C, (queries[0], keys[0], adapter[0]), [pltpu.VMEM((tok, W + Wk + 2 * R), bf)] * C))
        for s in range(1, C):
            msgs[s] = swap(msgs[s], s)
        by_dma = rblk % 128 == 0
        outs = [
            pltpu.VMEM(teacher.shape[1:], bf),
            pltpu.VMEM((R, W), bf),
            pltpu.VMEM((R, Wk), bf),
            pltpu.VMEM(pack.shape, jnp.int32),
            pltpu.VMEM(land.shape, jnp.int32),
        ] + [pltpu.VMEM((tok, E * rblk), bf)] * (4 if by_dma else 0)
        ins = (teacher[0], adapter_up.T, pack, land) + ((hidden[0],) if by_dma else ())
        teach, up_q, up_k, pack, land, *hids = slices(second_plan, 5 + (4 * E if by_dma else 0), ins, outs)
        if not by_dma:
            blocks = hidden[0].reshape(tok, C * Dp, rblk)
            me, me_d = lax.axis_index("ctx"), lax.axis_index("dp")
            hids = []
            for n in range(4):
                order = jnp.stack([column(me, me_d, n, e) // rblk for e in range(E)])
                hids.append(jnp.take(blocks, order, axis=1).reshape(tok, E * rblk))
        hids[1] = swap(hids[1], 1)
        hids[2] = swap(hids[2], 1, "dp")
        hids[3] = swap_diag(hids[3])

        smem = pl.BlockSpec(memory_space=pltpu.SMEM)
        vmem = pl.BlockSpec(memory_space=pltpu.VMEM)
        params = pltpu.CompilerParams(vmem_limit_bytes=24 * 2**20)
        low_rows, piece = C * R, slot // tok * R
        keep, send, own, even = pl.pallas_call(
            functools.partial(attend_kernel, C, tok, hq, kh, DH, H, R),
            out_shape=(
                pltpu.VMEM((C // 2, 2 * R, tok), f32),
                pltpu.VMEM((low_rows + 2 * piece, tok), f32),
                pltpu.VMEM((piece, tok), bf),
                pltpu.VMEM((piece, tok), bf),
            ),
            in_specs=[smem] + [vmem] * (C + 4),
            out_specs=tuple([vmem] * 4),
            scratch_shapes=[
                pltpu.VMEM((hq, S, DH), bf),
                pltpu.VMEM((S, Wk), bf),
                pltpu.VMEM((S, 2 * R), bf),
                pltpu.VMEM((S, W), bf),
                pltpu.VMEM((Wk, S), f32),
                pltpu.VMEM((2 * R, S), f32),
            ],
            compiler_params=params,
            name="attend",
        )(lengths, *[near(m) for m in msgs], near(teach), near(up_q), near(up_k), near(pack))

        pair = swap(send, 1)
        low = keep + pair[:low_rows].reshape(keep.shape)
        bit = 2
        while bit < C:
            both = low.reshape((-1, 2) + low.shape[1:])
            low = both[:, 0] + swap(both[:, 1].astype(bf), bit).astype(f32)
            bit *= 2
        relay = pair[low_rows + piece :].astype(bf)
        far = swap(jnp.concatenate([even, relay]), 1, "dp")
        low = low.astype(bf)
        low = jnp.concatenate([low, swap(low, 1, "dp")])
        other = swap(low, 1)

        send, keep = pl.pallas_call(
            functools.partial(down_kernel, R, rblk),
            out_shape=(pltpu.VMEM((E // 2, 3 * R, rblk), bf), pltpu.VMEM((E // 2, 3 * R, rblk), f32)),
            in_specs=[vmem] * 10,
            out_specs=(vmem, vmem),
            compiler_params=params,
            name="down",
        )(
            near(low), near(other), near(own), near(pair[low_rows : low_rows + piece]), near(far),
            *[near(h) for h in hids], near(land),
        )
        rounds = [("ctx", 2 << i) for i in range(C.bit_length() - 2)]
        rounds += [("dp", 2 << i) for i in range(Dp.bit_length() - 2)]
        for n, (axis, bit) in enumerate(rounds):
            if n:
                both = keep.reshape((-1, 2) + keep.shape[1:])
                keep, send = both[:, 0], both[:, 1].astype(bf)
            got = swap(send, bit, axis)
            if n < len(rounds) - 1:
                keep = keep + got.astype(f32)
        down, up = pl.pallas_call(
            functools.partial(final_kernel, R, rows_each),
            out_shape=(jax.ShapeDtypeStruct((rblk, 2 * R), f32), jax.ShapeDtypeStruct((R, rows_each), f32)),
            in_specs=[vmem, vmem],
            out_specs=(vmem, vmem),
            compiler_params=params,
            name="final",
        )(near(keep), near(got))
        return down, up.T

    placed = (
        P("dp", "ctx", None),
        P("dp", "ctx", None),
        P("dp", "ctx", None, None),
        P("dp"),
        P("dp", "ctx", None),
        P("dp", "ctx", None),
        P(),
    )
    return jax.shard_map(
        body,
        mesh=mesh,
        in_specs=placed,
        out_specs=(P(("dp", "ctx"), None), P(("dp", "ctx"), None)),
        check_vma=False,
    )
```

```python
import functools
import math

import jax
import jax.numpy as jnp
import numpy as np
from jax import lax
from jax.experimental import pallas as pl
from jax.experimental.pallas import tpu as pltpu
from jax.sharding import PartitionSpec as P

NT = (((1,), (1,)), ((), ()))
TN = (((0,), (0,)), ((), ()))


def dot32(a, b, dims=(((1,), (0,)), ((), ()))):
    return lax.dot_general(a, b, dims, preferred_element_type=jnp.float32)


def owner_tables(C, Dp, W, Wk, DH, q_width, group_cols, rows_total, lane_block, lanes):
    rows_each = rows_total // (C * Dp)
    local, groups = [], []
    for c in range(C):
        k_start = q_width + (c * W // group_cols) * DH
        local.append(np.concatenate([c * W + np.arange(W), k_start + np.arange(Wk)]))
        groups.append([np.nonzero(local[c] // rows_each // C % 4 == m)[0] for m in range(4)])
    slot = -(-max(len(g) for four in groups for g in four) // lanes) * lanes
    pack = np.full((C, 4, 4, slot), -1, np.int32)
    land = np.full((C, 4, slot), -1, np.int32)
    for c in range(C):
        for m in range(4):
            rows = local[c][groups[c][m]]
            owner = rows // rows_each
            land[c, m, : len(rows)] = (owner // C // 4 * C + owner % C) * lane_block + rows % rows_each
            for n in range(4):
                pack[c, m, n, : len(groups[c][m ^ n])] = groups[c][m ^ n]
    return pack.reshape(C * 4, 4 * slot), land.reshape(C * 4, slot), slot, rows_each


def slice_kernel(plan, n_in, *refs):
    ins, (*outs, sems) = refs[:n_in], refs[n_in:]
    copies = []
    for n, (i, src, o, dst, width) in enumerate(plan(lax.axis_index("ctx"), lax.axis_index("dp"))):
        source = ins[i] if src is None else ins[i].at[..., pl.ds(src, width)]
        target = outs[o] if dst is None else outs[o].at[..., pl.ds(dst, width)]
        copies.append(pltpu.make_async_copy(source, target, sems.at[n]))
    for c in copies:
        c.start()
    for c in copies:
        c.wait()


def slices(plan, count, ins, out_shapes):
    spec = pl.BlockSpec(memory_space=pltpu.HBM)
    vmem = pl.BlockSpec(memory_space=pltpu.VMEM)
    ins = [pltpu.with_memory_space_constraint(x, pltpu.HBM) for x in ins]
    return pl.pallas_call(
        functools.partial(slice_kernel, plan, len(ins)),
        out_shape=tuple(out_shapes),
        in_specs=[spec] * len(ins),
        out_specs=tuple([vmem] * len(out_shapes)),
        scratch_shapes=[pltpu.SemaphoreType.DMA((count,))],
        compiler_params=pltpu.CompilerParams(vmem_limit_bytes=2**20),
    )(*ins)


def attend_kernel(C, tok, hq, kh, DH, H, R, lengths, *refs):
    msgs = refs[:C]
    teacher, up_q, up_k = refs[C : C + 3]
    keep_out, send_out, dq_buf, dk_out, q_buf, k_buf, dk_buf, low_buf = refs[C + 3 :]
    me, length = lax.axis_index("ctx"), lengths[0]
    W = hq * DH
    per_key = hq // kh
    scale = 1.0 / math.sqrt(DH)
    exp_scale = scale * math.log2(math.e)
    for s in range(C):
        row = pl.multiple_of(jnp.bitwise_xor(me, s) * tok, tok)
        for h in range(hq):
            q_buf[h, pl.ds(row, tok), :] = msgs[s][:, h * DH : (h + 1) * DH]
        k_buf[pl.ds(row, tok), :] = msgs[s][:, W:]
    dk_buf[...] = jnp.zeros_like(dk_buf)
    row_in = lax.broadcasted_iota(jnp.int32, (tok, 1), 0)
    col_in = lax.broadcasted_iota(jnp.int32, (tok, tok), 1)
    for p in range(C):
        start, ext = p * tok, (p + 1) * tok
        row_pos = row_in + start
        visible = (col_in + start) <= jnp.minimum(row_pos, length - 1)
        weight = jnp.where(row_pos < length, 1.0 / H, 0.0)
        for g in range(kh):
            keys = k_buf[:ext, g * DH : (g + 1) * DH]
            heads = range(g * per_key, (g + 1) * per_key)
            q_all = q_buf[g * per_key : (g + 1) * per_key, start:ext, :].reshape(per_key * tok, DH)
            scores = dot32(q_all, keys, NT)
            grads = []
            for n, h in enumerate(heads):
                sc = scores[n * tok : (n + 1) * tok]
                diag = jnp.where(visible, sc[:, start:], -1e30)
                sc = diag if p == 0 else jnp.concatenate([sc[:, :start], diag], axis=1)
                te_d = jnp.where(visible, teacher[h, start:ext, start:ext].astype(jnp.float32), 0.0)
                te = te_d if p == 0 else jnp.concatenate(
                    [teacher[h, start:ext, :start].astype(jnp.float32), te_d], axis=1
                )
                ex = jnp.exp2((sc - jnp.max(sc, axis=1, keepdims=True)) * exp_scale)
                w_s = weight / jnp.sum(ex, axis=1, keepdims=True)
                w_t = weight / jnp.sum(te, axis=1, keepdims=True)
                grads.append((ex * w_s - te * w_t).astype(jnp.bfloat16))
            grad = grads[0] if per_key == 1 else jnp.concatenate(grads, axis=0)
            dq = (dot32(grad, keys) * scale).astype(jnp.bfloat16)
            for n, h in enumerate(heads):
                dq_buf[start:ext, h * DH : (h + 1) * DH] = dq[n * tok : (n + 1) * tok]
            dk_buf[g * DH : (g + 1) * DH, :ext] += dot32(q_all, grad, TN)
    dq = dq_buf[...]
    dk = (dk_buf[...] * scale).astype(jnp.bfloat16)
    dk_out[...] = dk
    low_buf[:R, :] = dot32(up_q[...], dq, NT)
    low_buf[R:, :] = dot32(up_k[...], dk)
    for s in range(C):
        pos = pl.multiple_of(jnp.bitwise_xor(me, s) * tok, tok)
        (send_out if s % 2 else keep_out)[s // 2] = low_buf[:, pl.ds(pos, tok)]


def up_kernel(C, tok, R, *refs):
    adapters = refs[:C]
    dq, dk, pack, keep, send, a_buf = refs[C:]
    me, me_d = lax.axis_index("ctx"), lax.axis_index("dp")
    for s in range(C):
        a_buf[pl.ds(pl.multiple_of(jnp.bitwise_xor(me, s) * tok, tok), tok), :] = adapters[s][...]
    a_q, a_k = a_buf[:, :R], a_buf[:, R:]
    grad_up = jnp.concatenate(
        [dot32(a_q, dq[...], TN).astype(jnp.bfloat16), dot32(a_k.T, dk[...], NT).astype(jnp.bfloat16)], axis=1
    )
    where_to = pack[pl.ds(me * 4 + jnp.bitwise_and(me_d, 3), 1), :]
    pick = lax.broadcasted_iota(jnp.int32, (grad_up.shape[1], where_to.shape[1]), 0) == where_to
    pick = jnp.where(pick, 1.0, 0.0).astype(jnp.bfloat16)
    rows = dot32(grad_up, pick)
    slot = where_to.shape[1] // 4
    for n in range(4):
        dst = send if n // 2 else keep
        dst[n % 2] = rows[:, n * slot : (n + 1) * slot].astype(dst.dtype)


def down_kernel(R, rblk, low_a, low_b, ups_a, ups_b, h0, h1, h2, h3, land, send, keep):
    acc = None
    for low, hid in zip((low_a[0], low_a[1], low_b[0], low_b[1]), (h0, h1, h2, h3)):
        term = dot32(low, hid[...])
        acc = term if acc is None else acc + term
    rows = (ups_a[...] + ups_b[...].astype(jnp.float32)).astype(jnp.bfloat16)
    me, me_d, width = lax.axis_index("ctx"), lax.axis_index("dp"), h0.shape[1]
    here = jnp.right_shift(me_d, 2) * lax.axis_size("ctx") + me
    where_to = jnp.bitwise_xor(land[pl.ds(me * 4 + jnp.bitwise_and(me_d, 3), 1), :], here * rblk)
    place = lax.broadcasted_iota(jnp.int32, (width, rows.shape[1]), 0) == where_to
    place = jnp.where(place, 1.0, 0.0).astype(jnp.bfloat16)
    ups = dot32(rows, place, NT)
    for e in range(width // rblk):
        dst = send if e % 2 else keep
        dst[e // 2, : 2 * R, :] = acc[:, e * rblk : (e + 1) * rblk].astype(dst.dtype)
        dst[e // 2, 2 * R :, :] = ups[:, e * rblk : (e + 1) * rblk].astype(dst.dtype)


def final_kernel(R, rows_each, kept, got, down, up):
    total = kept[0] + got[0].astype(jnp.float32)
    down[...] = total[: 2 * R].T
    up[...] = total[2 * R :, :rows_each]


def solution(mesh):
    C, Dp = mesh.shape["ctx"], mesh.shape["dp"]

    def swap(x, s, axis="ctx"):
        return lax.ppermute(x, axis, [(i, i ^ s) for i in range(mesh.shape[axis])])

    def near(x):
        return pltpu.with_memory_space_constraint(x, pltpu.VMEM)

    def body(queries, keys, teacher, lengths, hidden, adapter, adapter_up):
        tok = queries.shape[1]
        hq = teacher.shape[1]
        S = teacher.shape[2]
        H = hq * C
        DH = queries.shape[2] // H
        KV = keys.shape[2] // DH
        R = adapter.shape[2] // 2
        D = hidden.shape[2]
        q_width = H * DH
        rows_total = adapter_up.shape[0]
        kh = max(1, KV // C)
        W, Wk = hq * DH, kh * DH
        rblk = D // (C * Dp)
        group_cols = (H // KV) * DH
        bf, f32 = jnp.bfloat16, jnp.float32

        def key_col(dst):
            return (dst * W // group_cols) * DH

        def first_plan(me, me_d):
            for s in range(C):
                dst = jnp.bitwise_xor(me, s)
                yield 0, pl.multiple_of(dst * W, 128), s, 0, W
                yield 1, pl.multiple_of(key_col(dst), 128), s, W, Wk

        def second_plan(me, me_d):
            yield 0, None, 0, None, None
            yield 1, pl.multiple_of(me * W, 128), 1, 0, W
            yield 1, pl.multiple_of(q_width + key_col(me), 128), 2, 0, Wk
            yield 2, None, 3, None, None
            yield 3, None, 4, None, None
            if rblk % 128 == 0:
                for n in range(4):
                    for e in range(E):
                        yield 4, pl.multiple_of(column(me, me_d, n, e), 128), 5 + n, e * rblk, rblk

        E = C * Dp // 4

        def column(me, me_d, n, e):
            return (jnp.bitwise_xor(me_d, n + e // C * 4) * C + jnp.bitwise_xor(me, e % C)) * rblk

        pack, land, slot, rows_each = owner_tables(C, Dp, W, Wk, DH, q_width, group_cols, rows_total, rblk, tok)
        pack, land = jnp.asarray(pack), jnp.asarray(land)
        msgs = list(slices(first_plan, 2 * C, (queries[0], keys[0]), [pltpu.VMEM((tok, W + Wk), bf)] * C))
        for s in range(1, C):
            msgs[s] = swap(msgs[s], s)
        adapters = [adapter[0]] + [swap(adapter[0], s) for s in range(1, C)]
        by_dma = rblk % 128 == 0
        outs = [
            pltpu.VMEM(teacher.shape[1:], bf),
            pltpu.VMEM((R, W), bf),
            pltpu.VMEM((R, Wk), bf),
            pltpu.VMEM(pack.shape, jnp.int32),
            pltpu.VMEM(land.shape, jnp.int32),
        ] + [pltpu.VMEM((tok, E * rblk), bf)] * (4 if by_dma else 0)
        ins = (teacher[0], adapter_up.T, pack, land) + ((hidden[0],) if by_dma else ())
        teach, up_q, up_k, pack, land, *hids = slices(second_plan, 5 + (4 * E if by_dma else 0), ins, outs)
        if not by_dma:
            blocks = hidden[0].reshape(tok, C * Dp, rblk)
            me, me_d = lax.axis_index("ctx"), lax.axis_index("dp")
            hids = []
            for n in range(4):
                order = jnp.stack([column(me, me_d, n, e) // rblk for e in range(E)])
                hids.append(jnp.take(blocks, order, axis=1).reshape(tok, E * rblk))
        hids = [hids[0]] + [swap(hids[n], n, "dp") for n in range(1, 4)]

        smem = pl.BlockSpec(memory_space=pltpu.SMEM)
        vmem = pl.BlockSpec(memory_space=pltpu.VMEM)
        params = pltpu.CompilerParams(vmem_limit_bytes=24 * 2**20)
        keep, send, dq, dk = pl.pallas_call(
            functools.partial(attend_kernel, C, tok, hq, kh, DH, H, R),
            out_shape=(
                pltpu.VMEM((C // 2, 2 * R, tok), f32),
                pltpu.VMEM((C // 2, 2 * R, tok), f32),
                pltpu.VMEM((S, W), bf),
                pltpu.VMEM((Wk, S), bf),
            ),
            in_specs=[smem] + [vmem] * (C + 3),
            out_specs=tuple([vmem] * 4),
            scratch_shapes=[
                pltpu.VMEM((hq, S, DH), bf),
                pltpu.VMEM((S, Wk), bf),
                pltpu.VMEM((Wk, S), f32),
                pltpu.VMEM((2 * R, S), f32),
            ],
            compiler_params=params,
            name="attend",
        )(lengths, *[near(m) for m in msgs], near(teach), near(up_q), near(up_k))
        low = keep + swap(send, 1)
        bit = 2
        while bit < C:
            both = low.reshape((-1, 2) + low.shape[1:])
            low = both[:, 0] + swap(both[:, 1].astype(bf), bit).astype(f32)
            bit *= 2
        ups, send = pl.pallas_call(
            functools.partial(up_kernel, C, tok, R),
            out_shape=(pltpu.VMEM((2, R, slot), f32), pltpu.VMEM((2, R, slot), bf)),
            in_specs=[vmem] * (C + 3),
            out_specs=(vmem, vmem),
            scratch_shapes=[pltpu.VMEM((S, 2 * R), bf)],
            compiler_params=params,
            name="upgrad",
        )(*[near(a) for a in adapters], near(dq), near(dk), near(pack))
        ups = ups + swap(send, 2, "dp").astype(f32)
        low = low.astype(bf)
        low = jnp.concatenate([low, swap(low, 1, "dp")])
        got = swap(ups[1].astype(bf), 1, "dp")
        other = swap(low, 2, "dp")
        send, keep = pl.pallas_call(
            functools.partial(down_kernel, R, rblk),
            out_shape=(pltpu.VMEM((E // 2, 3 * R, rblk), bf), pltpu.VMEM((E // 2, 3 * R, rblk), f32)),
            in_specs=[vmem] * 9,
            out_specs=(vmem, vmem),
            compiler_params=params,
            name="down",
        )(*[near(x) for x in (low, other, ups[0], got, *hids, land)])
        rounds = [("ctx", 1 << i) for i in range(C.bit_length() - 1)]
        rounds += [("dp", 4 << i) for i in range(Dp.bit_length() - 3)]
        for n, (axis, bit) in enumerate(rounds):
            if n:
                both = keep.reshape((-1, 2) + keep.shape[1:])
                keep, send = both[:, 0], both[:, 1].astype(bf)
            got = swap(send, bit, axis)
            if n < len(rounds) - 1:
                keep = keep + got.astype(f32)
        down, up = pl.pallas_call(
            functools.partial(final_kernel, R, rows_each),
            out_shape=(jax.ShapeDtypeStruct((rblk, 2 * R), f32), jax.ShapeDtypeStruct((R, rows_each), f32)),
            in_specs=[vmem, vmem],
            out_specs=(vmem, vmem),
            compiler_params=params,
            name="final",
        )(near(keep), near(got))
        return down, up.T

    placed = (
        P("dp", "ctx", None),
        P("dp", "ctx", None),
        P("dp", "ctx", None, None),
        P("dp"),
        P("dp", "ctx", None),
        P("dp", "ctx", None),
        P(),
    )
    return jax.shard_map(
        body,
        mesh=mesh,
        in_specs=placed,
        out_specs=(P(("dp", "ctx"), None), P(("dp", "ctx"), None)),
        check_vma=False,
    )
```

```python
import functools
import math

import jax
import jax.numpy as jnp
import numpy as np
from jax import lax
from jax.experimental import pallas as pl
from jax.experimental.pallas import tpu as pltpu
from jax.sharding import PartitionSpec as P

NT = (((1,), (1,)), ((), ()))
TN = (((0,), (0,)), ((), ()))


def dot32(a, b, dims=(((1,), (0,)), ((), ()))):
    return lax.dot_general(a, b, dims, preferred_element_type=jnp.float32)


def owner_tables(C, Dp, W, Wk, DH, q_width, group_cols, rows_total, lane_block, lanes):
    rows_each = rows_total // (C * Dp)
    local, groups = [], []
    for c in range(C):
        k_start = q_width + (c * W // group_cols) * DH
        local.append(np.concatenate([c * W + np.arange(W), k_start + np.arange(Wk)]))
        groups.append([np.nonzero(local[c] // rows_each // C % 4 == m)[0] for m in range(4)])
    slot = -(-max(len(g) for four in groups for g in four) // lanes) * lanes
    pack = np.full((C, 4, 4, slot), -1, np.int32)
    land = np.full((C, 4, slot), -1, np.int32)
    for c in range(C):
        for m in range(4):
            rows = local[c][groups[c][m]]
            owner = rows // rows_each
            land[c, m, : len(rows)] = (owner // C // 4 * C + owner % C) * lane_block + rows % rows_each
            for n in range(4):
                pack[c, m, n, : len(groups[c][m ^ n])] = groups[c][m ^ n]
    return pack.reshape(C * 4, 4 * slot), land.reshape(C * 4, slot), slot, rows_each


def slice_kernel(plan, n_in, *refs):
    ins, (*outs, sems) = refs[:n_in], refs[n_in:]
    copies = []
    for n, (i, src, o, dst, width) in enumerate(plan(lax.axis_index("ctx"), lax.axis_index("dp"))):
        source = ins[i] if src is None else ins[i].at[..., pl.ds(src, width)]
        target = outs[o] if dst is None else outs[o].at[..., pl.ds(dst, width)]
        copies.append(pltpu.make_async_copy(source, target, sems.at[n]))
    for c in copies:
        c.start()
    for c in copies:
        c.wait()


def slices(plan, count, ins, out_shapes):
    spec = pl.BlockSpec(memory_space=pltpu.HBM)
    vmem = pl.BlockSpec(memory_space=pltpu.VMEM)
    ins = [pltpu.with_memory_space_constraint(x, pltpu.HBM) for x in ins]
    return pl.pallas_call(
        functools.partial(slice_kernel, plan, len(ins)),
        out_shape=tuple(out_shapes),
        in_specs=[spec] * len(ins),
        out_specs=tuple([vmem] * len(out_shapes)),
        scratch_shapes=[pltpu.SemaphoreType.DMA((count,))],
        compiler_params=pltpu.CompilerParams(vmem_limit_bytes=2**20),
    )(*ins)


def attend_kernel(C, tok, hq, kh, DH, H, R, lengths, *refs):
    msgs = refs[:C]
    teacher, up_q, up_k = refs[C : C + 3]
    keep_out, send_out, dq_buf, dk_out, q_buf, k_buf, dk_buf, low_buf = refs[C + 3 :]
    me, length = lax.axis_index("ctx"), lengths[0]
    W = hq * DH
    per_key = hq // kh
    scale = 1.0 / math.sqrt(DH)
    exp_scale = scale * math.log2(math.e)
    for s in range(C):
        row = pl.multiple_of(jnp.bitwise_xor(me, s) * tok, tok)
        for h in range(hq):
            q_buf[h, pl.ds(row, tok), :] = msgs[s][:, h * DH : (h + 1) * DH]
        k_buf[pl.ds(row, tok), :] = msgs[s][:, W : W + kh * DH]
    dk_buf[...] = jnp.zeros_like(dk_buf)
    row_in = lax.broadcasted_iota(jnp.int32, (tok, 1), 0)
    col_in = lax.broadcasted_iota(jnp.int32, (tok, tok), 1)
    for p in range(C):
        start, ext = p * tok, (p + 1) * tok
        row_pos = row_in + start
        visible = (col_in + start) <= jnp.minimum(row_pos, length - 1)
        weight = jnp.where(row_pos < length, 1.0 / H, 0.0)
        for g in range(kh):
            keys = k_buf[:ext, g * DH : (g + 1) * DH]
            heads = range(g * per_key, (g + 1) * per_key)
            q_all = q_buf[g * per_key : (g + 1) * per_key, start:ext, :].reshape(per_key * tok, DH)
            scores = dot32(q_all, keys, NT)
            grads = []
            for n, h in enumerate(heads):
                sc = scores[n * tok : (n + 1) * tok]
                diag = jnp.where(visible, sc[:, start:], -1e30)
                sc = diag if p == 0 else jnp.concatenate([sc[:, :start], diag], axis=1)
                te_d = jnp.where(visible, teacher[h, start:ext, start:ext].astype(jnp.float32), 0.0)
                te = te_d if p == 0 else jnp.concatenate(
                    [teacher[h, start:ext, :start].astype(jnp.float32), te_d], axis=1
                )
                ex = jnp.exp2((sc - jnp.max(sc, axis=1, keepdims=True)) * exp_scale)
                w_s = weight / jnp.sum(ex, axis=1, keepdims=True)
                w_t = weight / jnp.sum(te, axis=1, keepdims=True)
                grads.append((ex * w_s - te * w_t).astype(jnp.bfloat16))
            grad = grads[0] if per_key == 1 else jnp.concatenate(grads, axis=0)
            dq = (dot32(grad, keys) * scale).astype(jnp.bfloat16)
            for n, h in enumerate(heads):
                dq_buf[start:ext, h * DH : (h + 1) * DH] = dq[n * tok : (n + 1) * tok]
            dk_buf[g * DH : (g + 1) * DH, :ext] += dot32(q_all, grad, TN)
    dq = dq_buf[...]
    dk = (dk_buf[...] * scale).astype(jnp.bfloat16)
    dk_out[...] = dk
    low_buf[:R, :] = dot32(up_q[...], dq, NT)
    low_buf[R:, :] = dot32(up_k[...], dk)
    for s in range(C):
        pos = pl.multiple_of(jnp.bitwise_xor(me, s) * tok, tok)
        (send_out if s % 2 else keep_out)[s // 2] = low_buf[:, pl.ds(pos, tok)]


def up_kernel(C, tok, R, *refs):
    adapters, dq, dk, pack, keep, send, a_buf = refs
    me, me_d = lax.axis_index("ctx"), lax.axis_index("dp")
    for s in range(C):
        a_buf[pl.ds(pl.multiple_of(jnp.bitwise_xor(me, s) * tok, tok), tok), :] = adapters[s][...]
    a_q, a_k = a_buf[:, :R], a_buf[:, R:]
    grad_up = jnp.concatenate(
        [dot32(a_q, dq[...], TN).astype(jnp.bfloat16), dot32(a_k.T, dk[...], NT).astype(jnp.bfloat16)], axis=1
    )
    where_to = pack[pl.ds(me * 4 + jnp.bitwise_and(me_d, 3), 1), :]
    pick = lax.broadcasted_iota(jnp.int32, (grad_up.shape[1], where_to.shape[1]), 0) == where_to
    pick = jnp.where(pick, 1.0, 0.0).astype(jnp.bfloat16)
    rows = dot32(grad_up, pick)
    slot = where_to.shape[1] // 4
    for n in range(4):
        dst = send if n // 2 else keep
        dst[n % 2] = rows[:, n * slot : (n + 1) * slot].astype(dst.dtype)


def down_kernel(R, rblk, l0, l1, l2, l3, ups_a, ups_b, h0, h1, h2, h3, land, send, keep):
    acc = None
    for low, hid in zip((l0, l1, l2, l3), (h0, h1, h2, h3)):
        term = dot32(low[0], hid[...])
        acc = term if acc is None else acc + term
    rows = (ups_a[...] + ups_b[...].astype(jnp.float32)).astype(jnp.bfloat16)
    me, me_d, width = lax.axis_index("ctx"), lax.axis_index("dp"), h0.shape[1]
    here = jnp.right_shift(me_d, 2) * lax.axis_size("ctx") + me
    where_to = jnp.bitwise_xor(land[pl.ds(me * 4 + jnp.bitwise_and(me_d, 3), 1), :], here * rblk)
    place = lax.broadcasted_iota(jnp.int32, (width, rows.shape[1]), 0) == where_to
    place = jnp.where(place, 1.0, 0.0).astype(jnp.bfloat16)
    ups = dot32(rows, place, NT)
    for e in range(width // rblk):
        dst = send if e % 2 else keep
        dst[e // 2, : 2 * R, :] = acc[:, e * rblk : (e + 1) * rblk].astype(dst.dtype)
        dst[e // 2, 2 * R :, :] = ups[:, e * rblk : (e + 1) * rblk].astype(dst.dtype)


def final_kernel(R, rows_each, kept, got, down, up):
    total = kept[0] + got[0].astype(jnp.float32)
    down[...] = total[: 2 * R].T
    up[...] = total[2 * R :, :rows_each]


def solution(mesh):
    C, Dp = mesh.shape["ctx"], mesh.shape["dp"]

    def swap(x, s, axis="ctx"):
        return lax.ppermute(x, axis, [(i, i ^ s) for i in range(mesh.shape[axis])])

    def near(x):
        return pltpu.with_memory_space_constraint(x, pltpu.VMEM)

    def body(queries, keys, teacher, lengths, hidden, adapter, adapter_up):
        tok = queries.shape[1]
        hq = teacher.shape[1]
        S = teacher.shape[2]
        H = hq * C
        DH = queries.shape[2] // H
        KV = keys.shape[2] // DH
        R = adapter.shape[2] // 2
        D = hidden.shape[2]
        q_width = H * DH
        rows_total = adapter_up.shape[0]
        kh = max(1, KV // C)
        W, Wk = hq * DH, kh * DH
        rblk = D // (C * Dp)
        group_cols = (H // KV) * DH
        bf, f32 = jnp.bfloat16, jnp.float32

        def key_col(dst):
            return (dst * W // group_cols) * DH

        def first_plan(me, me_d):
            for s in range(C):
                dst = jnp.bitwise_xor(me, s)
                yield 0, pl.multiple_of(dst * W, 128), s, 0, W
                yield 1, pl.multiple_of(key_col(dst), 128), s, W, Wk
                if s < 2:
                    yield 2, 0, s, W + Wk, 2 * R

        def second_plan(me, me_d):
            yield 0, None, 0, None, None
            yield 1, pl.multiple_of(me * W, 128), 1, 0, W
            yield 1, pl.multiple_of(q_width + key_col(me), 128), 2, 0, Wk
            yield 2, None, 3, None, None
            yield 3, None, 4, None, None

        def hidden_plan(me, me_d):
            for n in range(4):
                for e in range(E):
                    yield 0, pl.multiple_of(column(me, me_d, n, e), 128), n, e * rblk, rblk

        E = C * Dp // 4

        def column(me, me_d, n, e):
            return (jnp.bitwise_xor(me_d, n + e // C * 4) * C + jnp.bitwise_xor(me, e % C)) * rblk

        pack, land, slot, rows_each = owner_tables(C, Dp, W, Wk, DH, q_width, group_cols, rows_total, rblk, tok)
        pack, land = jnp.asarray(pack), jnp.asarray(land)
        shapes = [pltpu.VMEM((tok, W + Wk + (2 * R if s < 2 else 0)), bf) for s in range(C)]
        msgs = list(slices(first_plan, 2 * C + 2, (queries[0], keys[0], adapter[0]), shapes))
        for s in range(1, C):
            msgs[s] = swap(msgs[s], s)
        if rblk % 128 == 0:
            hids = list(slices(hidden_plan, 4 * E, (hidden[0],), [pltpu.VMEM((tok, E * rblk), bf)] * 4))
        else:
            blocks = hidden[0].reshape(tok, C * Dp, rblk)
            me, me_d = lax.axis_index("ctx"), lax.axis_index("dp")
            hids = []
            for n in range(4):
                order = jnp.stack([column(me, me_d, n, e) // rblk for e in range(E)])
                hids.append(jnp.take(blocks, order, axis=1).reshape(tok, E * rblk))
        hids = [hids[0]] + [swap(hids[n], n, "dp") for n in range(1, 4)]
        adapters, bit = jnp.stack([m[:, W + Wk :] for m in msgs[:2]]), 2
        while bit < C:
            adapters = jnp.concatenate([adapters, swap(adapters, bit)])
            bit *= 2
        outs = [
            pltpu.VMEM(teacher.shape[1:], bf),
            pltpu.VMEM((R, W), bf),
            pltpu.VMEM((R, Wk), bf),
            pltpu.VMEM(pack.shape, jnp.int32),
            pltpu.VMEM(land.shape, jnp.int32),
        ]
        teach, up_q, up_k, pack, land = slices(second_plan, 5, (teacher[0], adapter_up.T, pack, land), outs)

        smem = pl.BlockSpec(memory_space=pltpu.SMEM)
        vmem = pl.BlockSpec(memory_space=pltpu.VMEM)
        params = pltpu.CompilerParams(vmem_limit_bytes=24 * 2**20)
        keep, send, dq, dk = pl.pallas_call(
            functools.partial(attend_kernel, C, tok, hq, kh, DH, H, R),
            out_shape=(
                pltpu.VMEM((C // 2, 2 * R, tok), f32),
                pltpu.VMEM((C // 2, 2 * R, tok), f32),
                pltpu.VMEM((S, W), bf),
                pltpu.VMEM((Wk, S), bf),
            ),
            in_specs=[smem] + [vmem] * (C + 3),
            out_specs=tuple([vmem] * 4),
            scratch_shapes=[
                pltpu.VMEM((hq, S, DH), bf),
                pltpu.VMEM((S, Wk), bf),
                pltpu.VMEM((Wk, S), f32),
                pltpu.VMEM((2 * R, S), f32),
            ],
            compiler_params=params,
            name="attend",
        )(lengths, *[near(m) for m in msgs], near(teach), near(up_q), near(up_k))
        low = keep + swap(send, 1)
        bit = 2
        while bit < C:
            both = low.reshape((-1, 2) + low.shape[1:])
            low = both[:, 0] + swap(both[:, 1].astype(bf), bit).astype(f32)
            bit *= 2
        ups, send = pl.pallas_call(
            functools.partial(up_kernel, C, tok, R),
            out_shape=(pltpu.VMEM((2, R, slot), f32), pltpu.VMEM((2, R, slot), bf)),
            in_specs=[vmem] * 4,
            out_specs=(vmem, vmem),
            scratch_shapes=[pltpu.VMEM((S, 2 * R), bf)],
            compiler_params=params,
            name="upgrad",
        )(near(adapters), near(dq), near(dk), near(pack))
        ups = ups + swap(send, 2, "dp").astype(f32)
        low = low.astype(bf)
        lows = [low] + [swap(low, n, "dp") for n in range(1, 4)]
        got = swap(ups[1].astype(bf), 1, "dp")
        send, keep = pl.pallas_call(
            functools.partial(down_kernel, R, rblk),
            out_shape=(pltpu.VMEM((E // 2, 3 * R, rblk), bf), pltpu.VMEM((E // 2, 3 * R, rblk), f32)),
            in_specs=[vmem] * 11,
            out_specs=(vmem, vmem),
            compiler_params=params,
            name="down",
        )(*[near(x) for x in (*lows, ups[0], got, *hids, land)])
        rounds = [("ctx", 1 << i) for i in range(C.bit_length() - 1)]
        rounds += [("dp", 4 << i) for i in range(Dp.bit_length() - 3)]
        for n, (axis, bit) in enumerate(rounds):
            if n:
                both = keep.reshape((-1, 2) + keep.shape[1:])
                keep, send = both[:, 0], both[:, 1].astype(bf)
            got = swap(send, bit, axis)
            if n < len(rounds) - 1:
                keep = keep + got.astype(f32)
        down, up = pl.pallas_call(
            functools.partial(final_kernel, R, rows_each),
            out_shape=(jax.ShapeDtypeStruct((rblk, 2 * R), f32), jax.ShapeDtypeStruct((R, rows_each), f32)),
            in_specs=[vmem, vmem],
            out_specs=(vmem, vmem),
            compiler_params=params,
            name="final",
        )(near(keep), near(got))
        return down, up.T

    placed = (
        P("dp", "ctx", None),
        P("dp", "ctx", None),
        P("dp", "ctx", None, None),
        P("dp"),
        P("dp", "ctx", None),
        P("dp", "ctx", None),
        P(),
    )
    return jax.shard_map(
        body,
        mesh=mesh,
        in_specs=placed,
        out_specs=(P(("dp", "ctx"), None), P(("dp", "ctx"), None)),
        check_vma=False,
    )
```

```python
import functools
import math

import jax
import jax.numpy as jnp
import numpy as np
from jax import lax
from jax.experimental import pallas as pl
from jax.experimental.pallas import tpu as pltpu
from jax.sharding import PartitionSpec as P

NT = (((1,), (1,)), ((), ()))
TN = (((0,), (0,)), ((), ()))


def dot32(a, b, dims=(((1,), (0,)), ((), ()))):
    return lax.dot_general(a, b, dims, preferred_element_type=jnp.float32)


def owner_tables(C, Dp, W, Wk, DH, q_width, group_cols, rows_total, lane_block, lanes):
    rows_each = rows_total // (C * Dp)
    local, groups = [], []
    for c in range(C):
        k_start = q_width + (c * W // group_cols) * DH
        local.append(np.concatenate([c * W + np.arange(W), k_start + np.arange(Wk)]))
        groups.append([np.nonzero(local[c] // rows_each // C % 4 == m)[0] for m in range(4)])
    slot = -(-max(len(g) for four in groups for g in four) // lanes) * lanes
    pack = np.full((C, 4, 4, slot), -1, np.int32)
    land = np.full((C, 4, slot), -1, np.int32)
    for c in range(C):
        for m in range(4):
            rows = local[c][groups[c][m]]
            owner = rows // rows_each
            land[c, m, : len(rows)] = (owner // C // 4 * C + owner % C) * lane_block + rows % rows_each
            for n in range(4):
                pack[c, m, n, : len(groups[c][m ^ n])] = groups[c][m ^ n]
    return pack.reshape(C * 4, 4 * slot), land.reshape(C * 4, slot), slot, rows_each


def slice_kernel(plan, n_in, *refs):
    ins, (*outs, sems) = refs[:n_in], refs[n_in:]
    copies = []
    for n, (i, src, o, dst, width) in enumerate(plan(lax.axis_index("ctx"), lax.axis_index("dp"))):
        source = ins[i] if src is None else ins[i].at[..., pl.ds(src, width)]
        target = outs[o] if dst is None else outs[o].at[..., pl.ds(dst, width)]
        copies.append(pltpu.make_async_copy(source, target, sems.at[n]))
    for c in copies:
        c.start()
    for c in copies:
        c.wait()


def slices(plan, count, ins, out_shapes):
    spec = pl.BlockSpec(memory_space=pltpu.HBM)
    vmem = pl.BlockSpec(memory_space=pltpu.VMEM)
    ins = [pltpu.with_memory_space_constraint(x, pltpu.HBM) for x in ins]
    return pl.pallas_call(
        functools.partial(slice_kernel, plan, len(ins)),
        out_shape=tuple(out_shapes),
        in_specs=[spec] * len(ins),
        out_specs=tuple([vmem] * len(out_shapes)),
        scratch_shapes=[pltpu.SemaphoreType.DMA((count,))],
        compiler_params=pltpu.CompilerParams(vmem_limit_bytes=2**20),
    )(*ins)


def attend_kernel(C, tok, hq, kh, DH, H, R, lengths, *refs):
    msgs = refs[:C]
    teacher, up_q, up_k = refs[C : C + 3]
    keep_out, send_out, dq_buf, dk_out, q_buf, k_buf, dk_buf, low_buf = refs[C + 3 :]
    me, length = lax.axis_index("ctx"), lengths[0]
    W = hq * DH
    per_key = hq // kh
    scale = 1.0 / math.sqrt(DH)
    exp_scale = scale * math.log2(math.e)
    for s in range(C):
        row = pl.multiple_of(jnp.bitwise_xor(me, s) * tok, tok)
        for h in range(hq):
            q_buf[h, pl.ds(row, tok), :] = msgs[s][:, h * DH : (h + 1) * DH]
        k_buf[pl.ds(row, tok), :] = msgs[s][:, W : W + kh * DH]
    dk_buf[...] = jnp.zeros_like(dk_buf)
    row_in = lax.broadcasted_iota(jnp.int32, (tok, 1), 0)
    col_in = lax.broadcasted_iota(jnp.int32, (tok, tok), 1)
    for p in range(C):
        start, ext = p * tok, (p + 1) * tok
        row_pos = row_in + start
        visible = (col_in + start) <= jnp.minimum(row_pos, length - 1)
        weight = jnp.where(row_pos < length, 1.0 / H, 0.0)
        for g in range(kh):
            keys = k_buf[:ext, g * DH : (g + 1) * DH]
            heads = range(g * per_key, (g + 1) * per_key)
            q_all = q_buf[g * per_key : (g + 1) * per_key, start:ext, :].reshape(per_key * tok, DH)
            scores = dot32(q_all, keys, NT)
            grads = []
            for n, h in enumerate(heads):
                sc = scores[n * tok : (n + 1) * tok]
                diag = jnp.where(visible, sc[:, start:], -1e30)
                sc = diag if p == 0 else jnp.concatenate([sc[:, :start], diag], axis=1)
                te_d = jnp.where(visible, teacher[h, start:ext, start:ext].astype(jnp.float32), 0.0)
                te = te_d if p == 0 else jnp.concatenate(
                    [teacher[h, start:ext, :start].astype(jnp.float32), te_d], axis=1
                )
                ex = jnp.exp2((sc - jnp.max(sc, axis=1, keepdims=True)) * exp_scale)
                w_s = weight / jnp.sum(ex, axis=1, keepdims=True)
                w_t = weight / jnp.sum(te, axis=1, keepdims=True)
                grads.append((ex * w_s - te * w_t).astype(jnp.bfloat16))
            grad = grads[0] if per_key == 1 else jnp.concatenate(grads, axis=0)
            dq = (dot32(grad, keys) * scale).astype(jnp.bfloat16)
            for n, h in enumerate(heads):
                dq_buf[start:ext, h * DH : (h + 1) * DH] = dq[n * tok : (n + 1) * tok]
            dk_buf[g * DH : (g + 1) * DH, :ext] += dot32(q_all, grad, TN)
    dq = dq_buf[...]
    dk = (dk_buf[...] * scale).astype(jnp.bfloat16)
    dk_out[...] = dk
    low_buf[:R, :] = dot32(up_q[...], dq, NT)
    low_buf[R:, :] = dot32(up_k[...], dk)
    for s in range(C):
        pos = pl.multiple_of(jnp.bitwise_xor(me, s) * tok, tok)
        (send_out if s % 2 else keep_out)[s // 2] = low_buf[:, pl.ds(pos, tok)]


def up_kernel(C, tok, R, *refs):
    adapters, dq, dk, pack, keep, send, a_buf = refs
    me, me_d = lax.axis_index("ctx"), lax.axis_index("dp")
    for s in range(C):
        a_buf[pl.ds(pl.multiple_of(jnp.bitwise_xor(me, s) * tok, tok), tok), :] = adapters[s][...]
    a_q, a_k = a_buf[:, :R], a_buf[:, R:]
    grad_up = jnp.concatenate(
        [dot32(a_q, dq[...], TN).astype(jnp.bfloat16), dot32(a_k.T, dk[...], NT).astype(jnp.bfloat16)], axis=1
    )
    where_to = pack[pl.ds(me * 4 + jnp.bitwise_and(me_d, 3), 1), :]
    pick = lax.broadcasted_iota(jnp.int32, (grad_up.shape[1], where_to.shape[1]), 0) == where_to
    pick = jnp.where(pick, 1.0, 0.0).astype(jnp.bfloat16)
    rows = dot32(grad_up, pick)
    slot = where_to.shape[1] // 4
    for n in range(4):
        dst = send if n // 2 else keep
        dst[n % 2] = rows[:, n * slot : (n + 1) * slot].astype(dst.dtype)


def down_kernel(R, rblk, l0, l1, l2, l3, ups_a, ups_b, h0, h1, h2, h3, land, send, keep):
    acc = None
    for low, hid in zip((l0, l1, l2, l3), (h0, h1, h2, h3)):
        term = dot32(low[0], hid[...])
        acc = term if acc is None else acc + term
    rows = (ups_a[...] + ups_b[...].astype(jnp.float32)).astype(jnp.bfloat16)
    me, me_d, width = lax.axis_index("ctx"), lax.axis_index("dp"), h0.shape[1]
    here = jnp.right_shift(me_d, 2) * lax.axis_size("ctx") + me
    where_to = jnp.bitwise_xor(land[pl.ds(me * 4 + jnp.bitwise_and(me_d, 3), 1), :], here * rblk)
    place = lax.broadcasted_iota(jnp.int32, (width, rows.shape[1]), 0) == where_to
    place = jnp.where(place, 1.0, 0.0).astype(jnp.bfloat16)
    ups = dot32(rows, place, NT)
    for e in range(width // rblk):
        dst = send if e % 2 else keep
        dst[e // 2, : 2 * R, :] = acc[:, e * rblk : (e + 1) * rblk].astype(dst.dtype)
        dst[e // 2, 2 * R :, :] = ups[:, e * rblk : (e + 1) * rblk].astype(dst.dtype)


def final_kernel(R, rows_each, kept, got, down, up):
    total = kept[0] + got[0].astype(jnp.float32)
    down[...] = total[: 2 * R].T
    up[...] = total[2 * R :, :rows_each]


def solution(mesh):
    C, Dp = mesh.shape["ctx"], mesh.shape["dp"]

    def swap(x, s, axis="ctx"):
        return lax.ppermute(x, axis, [(i, i ^ s) for i in range(mesh.shape[axis])])

    def near(x):
        return pltpu.with_memory_space_constraint(x, pltpu.VMEM)

    def body(queries, keys, teacher, lengths, hidden, adapter, adapter_up):
        tok = queries.shape[1]
        hq = teacher.shape[1]
        S = teacher.shape[2]
        H = hq * C
        DH = queries.shape[2] // H
        KV = keys.shape[2] // DH
        R = adapter.shape[2] // 2
        D = hidden.shape[2]
        q_width = H * DH
        rows_total = adapter_up.shape[0]
        kh = max(1, KV // C)
        W, Wk = hq * DH, kh * DH
        rblk = D // (C * Dp)
        group_cols = (H // KV) * DH
        bf, f32 = jnp.bfloat16, jnp.float32

        def key_col(dst):
            return (dst * W // group_cols) * DH

        def first_plan(me, me_d):
            for s in range(C):
                dst = jnp.bitwise_xor(me, s)
                yield 0, pl.multiple_of(dst * W, 128), s, 0, W
                yield 1, pl.multiple_of(key_col(dst), 128), s, W, Wk
                if s < 2:
                    yield 2, 0, s, W + Wk, 2 * R

        E = C * Dp // 4

        def column(me, me_d, n, e):
            return (jnp.bitwise_xor(me_d, n + e // C * 4) * C + jnp.bitwise_xor(me, e % C)) * rblk

        by_dma = rblk % 128 == 0

        def hidden_plan(me, me_d):
            for n in range(4):
                for e in range(E):
                    yield 0, pl.multiple_of(column(me, me_d, n, e), 128), n, e * rblk, rblk

        def second_plan(me, me_d):
            yield 0, None, 0, None, None
            yield 1, pl.multiple_of(me * W, 128), 1, 0, W
            yield 1, pl.multiple_of(q_width + key_col(me), 128), 2, 0, Wk
            yield 2, None, 3, None, None
            yield 3, None, 4, None, None

        pack, land, slot, rows_each = owner_tables(C, Dp, W, Wk, DH, q_width, group_cols, rows_total, rblk, tok)
        pack, land = jnp.asarray(pack), jnp.asarray(land)
        shapes = [pltpu.VMEM((tok, W + Wk + (2 * R if s < 2 else 0)), bf) for s in range(C)]
        msgs = list(slices(first_plan, 2 * C + 2, (queries[0], keys[0], adapter[0]), shapes))
        for s in range(1, C):
            msgs[s] = swap(msgs[s], s)
        if by_dma:
            hids = list(slices(hidden_plan, 4 * E, (hidden[0],), [pltpu.VMEM((tok, E * rblk), bf)] * 4))
        else:
            blocks, hids = hidden[0].reshape(tok, C * Dp, rblk), []
            me, me_d = lax.axis_index("ctx"), lax.axis_index("dp")
            for n in range(4):
                order = jnp.stack([column(me, me_d, n, e) // rblk for e in range(E)])
                hids.append(jnp.take(blocks, order, axis=1).reshape(tok, E * rblk))
        hids = [hids[0]] + [swap(hids[n], n, "dp") for n in range(1, 4)]
        adapters, bit = jnp.stack([m[:, W + Wk :] for m in msgs[:2]]), 2
        while bit < C:
            adapters = jnp.concatenate([adapters, swap(adapters, bit)])
            bit *= 2
        outs = [
            pltpu.VMEM(teacher.shape[1:], bf),
            pltpu.VMEM((R, W), bf),
            pltpu.VMEM((R, Wk), bf),
            pltpu.VMEM(pack.shape, jnp.int32),
            pltpu.VMEM(land.shape, jnp.int32),
        ]
        teach, up_q, up_k, pack, land = slices(second_plan, 5, (teacher[0], adapter_up.T, pack, land), outs)

        smem = pl.BlockSpec(memory_space=pltpu.SMEM)
        vmem = pl.BlockSpec(memory_space=pltpu.VMEM)
        params = pltpu.CompilerParams(vmem_limit_bytes=24 * 2**20)
        keep, send, dq, dk = pl.pallas_call(
            functools.partial(attend_kernel, C, tok, hq, kh, DH, H, R),
            out_shape=(
                pltpu.VMEM((C // 2, 2 * R, tok), f32),
                pltpu.VMEM((C // 2, 2 * R, tok), f32),
                pltpu.VMEM((S, W), bf),
                pltpu.VMEM((Wk, S), bf),
            ),
            in_specs=[smem] + [vmem] * (C + 3),
            out_specs=tuple([vmem] * 4),
            scratch_shapes=[
                pltpu.VMEM((hq, S, DH), bf),
                pltpu.VMEM((S, Wk), bf),
                pltpu.VMEM((Wk, S), f32),
                pltpu.VMEM((2 * R, S), f32),
            ],
            compiler_params=params,
            name="attend",
        )(lengths, *[near(m) for m in msgs], near(teach), near(up_q), near(up_k))
        low = keep + swap(send, 1)
        bit = 2
        while bit < C:
            both = low.reshape((-1, 2) + low.shape[1:])
            low = both[:, 0] + swap(both[:, 1].astype(bf), bit).astype(f32)
            bit *= 2
        ups, send = pl.pallas_call(
            functools.partial(up_kernel, C, tok, R),
            out_shape=(pltpu.VMEM((2, R, slot), f32), pltpu.VMEM((2, R, slot), bf)),
            in_specs=[vmem] * 4,
            out_specs=(vmem, vmem),
            scratch_shapes=[pltpu.VMEM((S, 2 * R), bf)],
            compiler_params=params,
            name="upgrad",
        )(near(adapters), near(dq), near(dk), near(pack))
        ups = ups + swap(send, 2, "dp").astype(f32)
        low = low.astype(bf)
        lows = [low]
        for n in range(1, 4):
            lows.append(swap(low, n, "dp"))
        got = swap(ups[1].astype(bf), 1, "dp")
        send, keep = pl.pallas_call(
            functools.partial(down_kernel, R, rblk),
            out_shape=(pltpu.VMEM((E // 2, 3 * R, rblk), bf), pltpu.VMEM((E // 2, 3 * R, rblk), f32)),
            in_specs=[vmem] * 11,
            out_specs=(vmem, vmem),
            compiler_params=params,
            name="down",
        )(*[near(x) for x in (*lows, ups[0], got, *hids, land)])
        rounds = [("ctx", 1 << i) for i in range(C.bit_length() - 1)]
        rounds += [("dp", 4 << i) for i in range(Dp.bit_length() - 3)]
        for n, (axis, bit) in enumerate(rounds):
            if n:
                both = keep.reshape((-1, 2) + keep.shape[1:])
                keep, send = both[:, 0], both[:, 1].astype(bf)
            got = swap(send, bit, axis)
            if n < len(rounds) - 1:
                keep = keep + got.astype(f32)
        down, up = pl.pallas_call(
            functools.partial(final_kernel, R, rows_each),
            out_shape=(jax.ShapeDtypeStruct((rblk, 2 * R), f32), jax.ShapeDtypeStruct((R, rows_each), f32)),
            in_specs=[vmem, vmem],
            out_specs=(vmem, vmem),
            compiler_params=params,
            name="final",
        )(near(keep), near(got))
        return down, up.T

    placed = (
        P("dp", "ctx", None),
        P("dp", "ctx", None),
        P("dp", "ctx", None, None),
        P("dp"),
        P("dp", "ctx", None),
        P("dp", "ctx", None),
        P(),
    )
    return jax.shard_map(
        body,
        mesh=mesh,
        in_specs=placed,
        out_specs=(P(("dp", "ctx"), None), P(("dp", "ctx"), None)),
        check_vma=False,
    )
```

```python
import functools
import math

import jax
import jax.numpy as jnp
import numpy as np
from jax import lax
from jax.experimental import pallas as pl
from jax.experimental.pallas import tpu as pltpu
from jax.sharding import PartitionSpec as P

NT = (((1,), (1,)), ((), ()))
TN = (((0,), (0,)), ((), ()))


def dot32(a, b, dims=(((1,), (0,)), ((), ()))):
    return lax.dot_general(a, b, dims, preferred_element_type=jnp.float32)


def owner_tables(C, Dp, W, Wk, DH, q_width, group_cols, rows_total, lane_block, lanes):
    rows_each = rows_total // (C * Dp)
    local, groups = [], []
    for c in range(C):
        k_start = q_width + (c * W // group_cols) * DH
        local.append(np.concatenate([c * W + np.arange(W), k_start + np.arange(Wk)]))
        groups.append([np.nonzero(local[c] // rows_each // C % 4 == m)[0] for m in range(4)])
    slot = -(-max(len(g) for four in groups for g in four) // lanes) * lanes
    pack = np.full((C, 4, 4, slot), -1, np.int32)
    land = np.full((C, 4, slot), -1, np.int32)
    for c in range(C):
        for m in range(4):
            rows = local[c][groups[c][m]]
            owner = rows // rows_each
            land[c, m, : len(rows)] = (owner // C // 4 * C + owner % C) * lane_block + rows % rows_each
            for n in range(4):
                pack[c, m, n, : len(groups[c][m ^ n])] = groups[c][m ^ n]
    return pack.reshape(C * 4, 4 * slot), land.reshape(C * 4, slot), slot, rows_each


def slice_kernel(plan, n_in, *refs):
    ins, (*outs, sems) = refs[:n_in], refs[n_in:]
    copies = []
    for n, (i, src, o, dst, width) in enumerate(plan(lax.axis_index("ctx"), lax.axis_index("dp"))):
        source = ins[i] if src is None else ins[i].at[..., pl.ds(src, width)]
        target = outs[o] if dst is None else outs[o].at[..., pl.ds(dst, width)]
        copies.append(pltpu.make_async_copy(source, target, sems.at[n]))
    for c in copies:
        c.start()
    for c in copies:
        c.wait()


def slices(plan, count, ins, out_shapes):
    spec = pl.BlockSpec(memory_space=pltpu.HBM)
    vmem = pl.BlockSpec(memory_space=pltpu.VMEM)
    ins = [pltpu.with_memory_space_constraint(x, pltpu.HBM) for x in ins]
    return pl.pallas_call(
        functools.partial(slice_kernel, plan, len(ins)),
        out_shape=tuple(out_shapes),
        in_specs=[spec] * len(ins),
        out_specs=tuple([vmem] * len(out_shapes)),
        scratch_shapes=[pltpu.SemaphoreType.DMA((count,))],
        compiler_params=pltpu.CompilerParams(vmem_limit_bytes=2**20),
    )(*ins)


def attend_kernel(C, tok, hq, kh, DH, H, R, lengths, *refs):
    msgs = refs[:C]
    teacher, up_q, up_k = refs[C : C + 3]
    keep_out, send_out, dq_buf, dk_out, q_buf, k_buf, dk_buf, low_buf = refs[C + 3 :]
    me, length = lax.axis_index("ctx"), lengths[0]
    W = hq * DH
    per_key = hq // kh
    scale = 1.0 / math.sqrt(DH)
    exp_scale = scale * math.log2(math.e)
    for s in range(C):
        row = pl.multiple_of(jnp.bitwise_xor(me, s) * tok, tok)
        for h in range(hq):
            q_buf[h, pl.ds(row, tok), :] = msgs[s][:, h * DH : (h + 1) * DH]
        k_buf[pl.ds(row, tok), :] = msgs[s][:, W : W + kh * DH]
    dk_buf[...] = jnp.zeros_like(dk_buf)
    row_in = lax.broadcasted_iota(jnp.int32, (tok, 1), 0)
    col_in = lax.broadcasted_iota(jnp.int32, (tok, tok), 1)

    def scores_of(p, g):
        start, ext = p * tok, (p + 1) * tok
        q_all = q_buf[g * per_key : (g + 1) * per_key, start:ext, :].reshape(per_key * tok, DH)
        return q_all, dot32(q_all, k_buf[:ext, g * DH : (g + 1) * DH], NT)

    def grads_of(p, g, scores):
        start, ext = p * tok, (p + 1) * tok
        row_pos = row_in + start
        visible = (col_in + start) <= jnp.minimum(row_pos, length - 1)
        weight = jnp.where(row_pos < length, 1.0 / H, 0.0)
        grads = []
        for n in range(per_key):
            h = g * per_key + n
            sc = scores[n * tok : (n + 1) * tok]
            diag = jnp.where(visible, sc[:, start:], -1e30)
            sc = diag if p == 0 else jnp.concatenate([sc[:, :start], diag], axis=1)
            te_d = jnp.where(visible, teacher[h, start:ext, start:ext].astype(jnp.float32), 0.0)
            te = te_d if p == 0 else jnp.concatenate(
                [teacher[h, start:ext, :start].astype(jnp.float32), te_d], axis=1
            )
            ex = jnp.exp2((sc - jnp.max(sc, axis=1, keepdims=True)) * exp_scale)
            w_s = weight / jnp.sum(ex, axis=1, keepdims=True)
            w_t = weight / jnp.sum(te, axis=1, keepdims=True)
            grads.append((ex * w_s - te * w_t).astype(jnp.bfloat16))
        return grads[0] if per_key == 1 else jnp.concatenate(grads, axis=0)

    def products_of(p, g, q_all, grad):
        start, ext = p * tok, (p + 1) * tok
        dq = (dot32(grad, k_buf[:ext, g * DH : (g + 1) * DH]) * scale).astype(jnp.bfloat16)
        for n in range(per_key):
            h = g * per_key + n
            dq_buf[start:ext, h * DH : (h + 1) * DH] = dq[n * tok : (n + 1) * tok]
        dk_buf[g * DH : (g + 1) * DH, :ext] += dot32(q_all, grad, TN)

    steps = [(p, g) for p in reversed(range(C)) for g in range(kh)]
    lag, ready, done = 1, {}, {}
    for i in range(len(steps) + 2 * lag):
        if i < len(steps):
            ready[i] = scores_of(*steps[i])
        j = i - lag
        if 0 <= j < len(steps):
            q_all, scores = ready.pop(j)
            done[j] = q_all, grads_of(*steps[j], scores)
        j = i - 2 * lag
        if 0 <= j < len(steps):
            products_of(*steps[j], *done.pop(j))
    dq = dq_buf[...]
    dk = (dk_buf[...] * scale).astype(jnp.bfloat16)
    dk_out[...] = dk
    low_buf[:R, :] = dot32(up_q[...], dq, NT)
    low_buf[R:, :] = dot32(up_k[...], dk)
    for s in range(C):
        pos = pl.multiple_of(jnp.bitwise_xor(me, s) * tok, tok)
        (send_out if s % 2 else keep_out)[s // 2] = low_buf[:, pl.ds(pos, tok)]


def up_kernel(C, tok, R, *refs):
    adapters, dq, dk, pack, keep, send, a_buf = refs
    me, me_d = lax.axis_index("ctx"), lax.axis_index("dp")
    for s in range(C):
        a_buf[pl.ds(pl.multiple_of(jnp.bitwise_xor(me, s) * tok, tok), tok), :] = adapters[s][...]
    a_q, a_k = a_buf[:, :R], a_buf[:, R:]
    grad_up = jnp.concatenate(
        [dot32(a_q, dq[...], TN).astype(jnp.bfloat16), dot32(a_k.T, dk[...], NT).astype(jnp.bfloat16)], axis=1
    )
    where_to = pack[pl.ds(me * 4 + jnp.bitwise_and(me_d, 3), 1), :]
    pick = lax.broadcasted_iota(jnp.int32, (grad_up.shape[1], where_to.shape[1]), 0) == where_to
    pick = jnp.where(pick, 1.0, 0.0).astype(jnp.bfloat16)
    rows = dot32(grad_up, pick)
    slot = where_to.shape[1] // 4
    for n in range(4):
        dst = send if n // 2 else keep
        dst[n % 2] = rows[:, n * slot : (n + 1) * slot].astype(dst.dtype)


def down_kernel(R, rblk, l0, l1, l2, l3, ups_a, ups_b, h0, h1, h2, h3, land, send, keep):
    acc = None
    for low, hid in zip((l0, l1, l2, l3), (h0, h1, h2, h3)):
        term = dot32(low[0], hid[...])
        acc = term if acc is None else acc + term
    rows = (ups_a[...] + ups_b[...].astype(jnp.float32)).astype(jnp.bfloat16)
    me, me_d, width = lax.axis_index("ctx"), lax.axis_index("dp"), h0.shape[1]
    here = jnp.right_shift(me_d, 2) * lax.axis_size("ctx") + me
    where_to = jnp.bitwise_xor(land[pl.ds(me * 4 + jnp.bitwise_and(me_d, 3), 1), :], here * rblk)
    place = lax.broadcasted_iota(jnp.int32, (width, rows.shape[1]), 0) == where_to
    place = jnp.where(place, 1.0, 0.0).astype(jnp.bfloat16)
    ups = dot32(rows, place, NT)
    for e in range(width // rblk):
        dst = send if e % 2 else keep
        dst[e // 2, : 2 * R, :] = acc[:, e * rblk : (e + 1) * rblk].astype(dst.dtype)
        dst[e // 2, 2 * R :, :] = ups[:, e * rblk : (e + 1) * rblk].astype(dst.dtype)


def final_kernel(R, rows_each, kept, got, down, up):
    total = kept[0] + got[0].astype(jnp.float32)
    down[...] = total[: 2 * R].T
    up[...] = total[2 * R :, :rows_each]


def solution(mesh):
    C, Dp = mesh.shape["ctx"], mesh.shape["dp"]

    def swap(x, s, axis="ctx"):
        return lax.ppermute(x, axis, [(i, i ^ s) for i in range(mesh.shape[axis])])

    def near(x):
        return pltpu.with_memory_space_constraint(x, pltpu.VMEM)

    def body(queries, keys, teacher, lengths, hidden, adapter, adapter_up):
        tok = queries.shape[1]
        hq = teacher.shape[1]
        S = teacher.shape[2]
        H = hq * C
        DH = queries.shape[2] // H
        KV = keys.shape[2] // DH
        R = adapter.shape[2] // 2
        D = hidden.shape[2]
        q_width = H * DH
        rows_total = adapter_up.shape[0]
        kh = max(1, KV // C)
        W, Wk = hq * DH, kh * DH
        rblk = D // (C * Dp)
        group_cols = (H // KV) * DH
        bf, f32 = jnp.bfloat16, jnp.float32

        def key_col(dst):
            return (dst * W // group_cols) * DH

        def first_plan(me, me_d):
            for s in range(C):
                dst = jnp.bitwise_xor(me, s)
                yield 0, pl.multiple_of(dst * W, 128), s, 0, W
                yield 1, pl.multiple_of(key_col(dst), 128), s, W, Wk
                if s < 2:
                    yield 2, 0, s, W + Wk, 2 * R

        E = C * Dp // 4

        def column(me, me_d, n, e):
            return (jnp.bitwise_xor(me_d, n + e // C * 4) * C + jnp.bitwise_xor(me, e % C)) * rblk

        by_dma = rblk % 128 == 0

        def hidden_plan(me, me_d):
            for n in range(4):
                for e in range(E):
                    yield 0, pl.multiple_of(column(me, me_d, n, e), 128), n, e * rblk, rblk

        def second_plan(me, me_d):
            yield 0, None, 0, None, None
            yield 1, pl.multiple_of(me * W, 128), 1, 0, W
            yield 1, pl.multiple_of(q_width + key_col(me), 128), 2, 0, Wk
            yield 2, None, 3, None, None
            yield 3, None, 4, None, None

        pack, land, slot, rows_each = owner_tables(C, Dp, W, Wk, DH, q_width, group_cols, rows_total, rblk, tok)
        pack, land = jnp.asarray(pack), jnp.asarray(land)
        shapes = [pltpu.VMEM((tok, W + Wk + (2 * R if s < 2 else 0)), bf) for s in range(C)]
        msgs = list(slices(first_plan, 2 * C + 2, (queries[0], keys[0], adapter[0]), shapes))
        for s in range(1, C):
            msgs[s] = swap(msgs[s], s)
        if by_dma:
            hids = list(slices(hidden_plan, 4 * E, (hidden[0],), [pltpu.VMEM((tok, E * rblk), bf)] * 4))
        else:
            blocks, hids = hidden[0].reshape(tok, C * Dp, rblk), []
            me, me_d = lax.axis_index("ctx"), lax.axis_index("dp")
            for n in range(4):
                order = jnp.stack([column(me, me_d, n, e) // rblk for e in range(E)])
                hids.append(jnp.take(blocks, order, axis=1).reshape(tok, E * rblk))
        hids = [hids[0]] + [swap(hids[n], n, "dp") for n in range(1, 4)]
        adapters, bit = jnp.stack([m[:, W + Wk :] for m in msgs[:2]]), 2
        while bit < C:
            adapters = jnp.concatenate([adapters, swap(adapters, bit)])
            bit *= 2
        outs = [
            pltpu.VMEM(teacher.shape[1:], bf),
            pltpu.VMEM((R, W), bf),
            pltpu.VMEM((R, Wk), bf),
            pltpu.VMEM(pack.shape, jnp.int32),
            pltpu.VMEM(land.shape, jnp.int32),
        ]
        teach, up_q, up_k, pack, land = slices(second_plan, 5, (teacher[0], adapter_up.T, pack, land), outs)

        smem = pl.BlockSpec(memory_space=pltpu.SMEM)
        vmem = pl.BlockSpec(memory_space=pltpu.VMEM)
        params = pltpu.CompilerParams(vmem_limit_bytes=24 * 2**20)
        keep, send, dq, dk = pl.pallas_call(
            functools.partial(attend_kernel, C, tok, hq, kh, DH, H, R),
            out_shape=(
                pltpu.VMEM((C // 2, 2 * R, tok), f32),
                pltpu.VMEM((C // 2, 2 * R, tok), f32),
                pltpu.VMEM((S, W), bf),
                pltpu.VMEM((Wk, S), bf),
            ),
            in_specs=[smem] + [vmem] * (C + 3),
            out_specs=tuple([vmem] * 4),
            scratch_shapes=[
                pltpu.VMEM((hq, S, DH), bf),
                pltpu.VMEM((S, Wk), bf),
                pltpu.VMEM((Wk, S), f32),
                pltpu.VMEM((2 * R, S), f32),
            ],
            compiler_params=params,
            name="attend",
        )(lengths, *[near(m) for m in msgs], near(teach), near(up_q), near(up_k))
        low = keep + swap(send, 1)
        bit = 2
        while bit < C:
            both = low.reshape((-1, 2) + low.shape[1:])
            low = both[:, 0] + swap(both[:, 1].astype(bf), bit).astype(f32)
            bit *= 2
        ups, send = pl.pallas_call(
            functools.partial(up_kernel, C, tok, R),
            out_shape=(pltpu.VMEM((2, R, slot), f32), pltpu.VMEM((2, R, slot), bf)),
            in_specs=[vmem] * 4,
            out_specs=(vmem, vmem),
            scratch_shapes=[pltpu.VMEM((S, 2 * R), bf)],
            compiler_params=params,
            name="upgrad",
        )(near(adapters), near(dq), near(dk), near(pack))
        ups = ups + swap(send, 2, "dp").astype(f32)
        low = low.astype(bf)
        lows = [low]
        for n in range(1, 4):
            lows.append(swap(low, n, "dp"))
        got = swap(ups[1].astype(bf), 1, "dp")
        send, keep = pl.pallas_call(
            functools.partial(down_kernel, R, rblk),
            out_shape=(pltpu.VMEM((E // 2, 3 * R, rblk), bf), pltpu.VMEM((E // 2, 3 * R, rblk), f32)),
            in_specs=[vmem] * 11,
            out_specs=(vmem, vmem),
            compiler_params=params,
            name="down",
        )(*[near(x) for x in (*lows, ups[0], got, *hids, land)])
        rounds = [("ctx", 1 << i) for i in range(C.bit_length() - 1)]
        rounds += [("dp", 4 << i) for i in range(Dp.bit_length() - 3)]
        for n, (axis, bit) in enumerate(rounds):
            if n:
                both = keep.reshape((-1, 2) + keep.shape[1:])
                keep, send = both[:, 0], both[:, 1].astype(bf)
            got = swap(send, bit, axis)
            if n < len(rounds) - 1:
                keep = keep + got.astype(f32)
        down, up = pl.pallas_call(
            functools.partial(final_kernel, R, rows_each),
            out_shape=(jax.ShapeDtypeStruct((rblk, 2 * R), f32), jax.ShapeDtypeStruct((R, rows_each), f32)),
            in_specs=[vmem, vmem],
            out_specs=(vmem, vmem),
            compiler_params=params,
            name="final",
        )(near(keep), near(got))
        return down, up.T

    placed = (
        P("dp", "ctx", None),
        P("dp", "ctx", None),
        P("dp", "ctx", None, None),
        P("dp"),
        P("dp", "ctx", None),
        P("dp", "ctx", None),
        P(),
    )
    return jax.shard_map(
        body,
        mesh=mesh,
        in_specs=placed,
        out_specs=(P(("dp", "ctx"), None), P(("dp", "ctx"), None)),
        check_vma=False,
    )
```

```python
import functools
import math

import jax
import jax.numpy as jnp
import numpy as np
from jax import lax
from jax.experimental import pallas as pl
from jax.experimental.pallas import tpu as pltpu
from jax.sharding import PartitionSpec as P

NT = (((1,), (1,)), ((), ()))
TN = (((0,), (0,)), ((), ()))


def dot32(a, b, dims=(((1,), (0,)), ((), ()))):
    return lax.dot_general(a, b, dims, preferred_element_type=jnp.float32)


def owner_tables(C, Dp, W, Wk, DH, q_width, group_cols, rows_total, lane_block, lanes):
    rows_each = rows_total // (C * Dp)
    local, groups = [], []
    for c in range(C):
        k_start = q_width + (c * W // group_cols) * DH
        local.append(np.concatenate([c * W + np.arange(W), k_start + np.arange(Wk)]))
        groups.append([np.nonzero(local[c] // rows_each // C % 4 == m)[0] for m in range(4)])
    slot = -(-max(len(g) for four in groups for g in four) // lanes) * lanes
    pack = np.full((C, 4, 4, slot), -1, np.int32)
    land = np.full((C, 4, slot), -1, np.int32)
    for c in range(C):
        for m in range(4):
            rows = local[c][groups[c][m]]
            owner = rows // rows_each
            land[c, m, : len(rows)] = (owner // C // 4 * C + owner % C) * lane_block + rows % rows_each
            for n in range(4):
                pack[c, m, n, : len(groups[c][m ^ n])] = groups[c][m ^ n]
    return pack.reshape(C * 4, 4 * slot), land.reshape(C * 4, slot), slot, rows_each


def slice_kernel(plan, n_in, *refs):
    ins, (*outs, sems) = refs[:n_in], refs[n_in:]
    copies = []
    for n, (i, src, o, dst, width) in enumerate(plan(lax.axis_index("ctx"), lax.axis_index("dp"))):
        source = ins[i] if src is None else ins[i].at[..., pl.ds(src, width)]
        target = outs[o] if dst is None else outs[o].at[..., pl.ds(dst, width)]
        copies.append(pltpu.make_async_copy(source, target, sems.at[n]))
    for c in copies:
        c.start()
    for c in copies:
        c.wait()


def slices(plan, count, ins, out_shapes):
    spec = pl.BlockSpec(memory_space=pltpu.HBM)
    vmem = pl.BlockSpec(memory_space=pltpu.VMEM)
    ins = [pltpu.with_memory_space_constraint(x, pltpu.HBM) for x in ins]
    return pl.pallas_call(
        functools.partial(slice_kernel, plan, len(ins)),
        out_shape=tuple(out_shapes),
        in_specs=[spec] * len(ins),
        out_specs=tuple([vmem] * len(out_shapes)),
        scratch_shapes=[pltpu.SemaphoreType.DMA((count,))],
        compiler_params=pltpu.CompilerParams(vmem_limit_bytes=2**20),
    )(*ins)


def attend_kernel(C, tok, hq, kh, DH, H, R, lengths, *refs):
    msgs = refs[:C]
    teacher, up_q, up_k = refs[C : C + 3]
    keep_out, send_out, dq_buf, dk_out, q_buf, k_buf, dk_buf, low_buf = refs[C + 3 :]
    me, length = lax.axis_index("ctx"), lengths[0]
    W = hq * DH
    per_key = hq // kh
    scale = 1.0 / math.sqrt(DH)
    exp_scale = scale * math.log2(math.e)
    for s in range(C):
        row = pl.multiple_of(jnp.bitwise_xor(me, s) * tok, tok)
        for h in range(hq):
            q_buf[h, pl.ds(row, tok), :] = msgs[s][:, h * DH : (h + 1) * DH]
        k_buf[pl.ds(row, tok), :] = msgs[s][:, W : W + kh * DH]
    dk_buf[...] = jnp.zeros_like(dk_buf)
    row_in = lax.broadcasted_iota(jnp.int32, (tok, 1), 0)
    col_in = lax.broadcasted_iota(jnp.int32, (tok, tok), 1)

    def scores_of(p, g):
        start, ext = p * tok, (p + 1) * tok
        q_all = q_buf[g * per_key : (g + 1) * per_key, start:ext, :].reshape(per_key * tok, DH)
        return q_all, dot32(q_all, k_buf[:ext, g * DH : (g + 1) * DH], NT)

    def grads_of(p, g, scores):
        start, ext = p * tok, (p + 1) * tok
        row_pos = row_in + start
        visible = (col_in + start) <= jnp.minimum(row_pos, length - 1)
        weight = jnp.where(row_pos < length, 1.0 / H, 0.0)
        grads = []
        for n in range(per_key):
            h = g * per_key + n
            sc = scores[n * tok : (n + 1) * tok]
            diag = jnp.where(visible, sc[:, start:], -1e30)
            sc = diag if p == 0 else jnp.concatenate([sc[:, :start], diag], axis=1)
            te_d = jnp.where(visible, teacher[h, start:ext, start:ext].astype(jnp.float32), 0.0)
            te = te_d if p == 0 else jnp.concatenate(
                [teacher[h, start:ext, :start].astype(jnp.float32), te_d], axis=1
            )
            ex = jnp.exp2((sc - jnp.max(sc, axis=1, keepdims=True)) * exp_scale)
            w_s = weight / jnp.sum(ex, axis=1, keepdims=True)
            w_t = weight / jnp.sum(te, axis=1, keepdims=True)
            grads.append((ex * w_s - te * w_t).astype(jnp.bfloat16))
        return grads[0] if per_key == 1 else jnp.concatenate(grads, axis=0)

    def products_of(p, g, q_all, grad):
        start, ext = p * tok, (p + 1) * tok
        dq = (dot32(grad, k_buf[:ext, g * DH : (g + 1) * DH]) * scale).astype(jnp.bfloat16)
        for n in range(per_key):
            h = g * per_key + n
            dq_buf[start:ext, h * DH : (h + 1) * DH] = dq[n * tok : (n + 1) * tok]
        dk_buf[g * DH : (g + 1) * DH, :ext] += dot32(q_all, grad, TN)

    steps = [(p, g) for p in reversed(range(C)) for g in range(kh)]
    lag, ready, done = 1, {}, {}
    for i in range(len(steps) + 2 * lag):
        if i < len(steps):
            ready[i] = scores_of(*steps[i])
        j = i - lag
        if 0 <= j < len(steps):
            q_all, scores = ready.pop(j)
            done[j] = q_all, grads_of(*steps[j], scores)
        j = i - 2 * lag
        if 0 <= j < len(steps):
            products_of(*steps[j], *done.pop(j))
    dq = dq_buf[...]
    dk = (dk_buf[...] * scale).astype(jnp.bfloat16)
    dk_out[...] = dk
    low_buf[:R, :] = dot32(up_q[...], dq, NT)
    low_buf[R:, :] = dot32(up_k[...], dk)
    for s in range(C):
        pos = pl.multiple_of(jnp.bitwise_xor(me, s) * tok, tok)
        (send_out if s % 2 else keep_out)[s // 2] = low_buf[:, pl.ds(pos, tok)]


def up_kernel(C, tok, R, *refs):
    adapters, dq, dk, pack, keep, send, a_buf = refs
    me, me_d = lax.axis_index("ctx"), lax.axis_index("dp")
    for s in range(C):
        a_buf[pl.ds(pl.multiple_of(jnp.bitwise_xor(me, s) * tok, tok), tok), :] = adapters[s][...]
    a_q, a_k = a_buf[:, :R], a_buf[:, R:]
    grad_up = jnp.concatenate(
        [dot32(a_q, dq[...], TN).astype(jnp.bfloat16), dot32(a_k.T, dk[...], NT).astype(jnp.bfloat16)], axis=1
    )
    where_to = pack[pl.ds(me * 4 + jnp.bitwise_and(me_d, 3), 1), :]
    pick = lax.broadcasted_iota(jnp.int32, (grad_up.shape[1], where_to.shape[1]), 0) == where_to
    pick = jnp.where(pick, 1.0, 0.0).astype(jnp.bfloat16)
    rows = dot32(grad_up, pick)
    slot = where_to.shape[1] // 4
    for n in range(4):
        dst = send if n // 2 else keep
        dst[n % 2] = rows[:, n * slot : (n + 1) * slot].astype(dst.dtype)


def down_kernel(rblk, l0, l1, l2, l3, h0, h1, h2, h3, send, keep):
    acc = None
    for low, hid in zip((l0, l1, l2, l3), (h0, h1, h2, h3)):
        term = dot32(low[0], hid[...])
        acc = term if acc is None else acc + term
    for e in range(h0.shape[1] // rblk):
        dst = send if e % 2 else keep
        dst[e // 2] = acc[:, e * rblk : (e + 1) * rblk].astype(dst.dtype)


def place_kernel(rblk, ups_a, ups_b, land, send, keep):
    rows = (ups_a[...] + ups_b[...].astype(jnp.float32)).astype(jnp.bfloat16)
    me, me_d, blocks = lax.axis_index("ctx"), lax.axis_index("dp"), 2 * keep.shape[0]
    here = jnp.right_shift(me_d, 2) * lax.axis_size("ctx") + me
    where_to = jnp.bitwise_xor(land[pl.ds(me * 4 + jnp.bitwise_and(me_d, 3), 1), :], here * rblk)
    place = lax.broadcasted_iota(jnp.int32, (blocks * rblk, rows.shape[1]), 0) == where_to
    place = jnp.where(place, 1.0, 0.0).astype(jnp.bfloat16)
    ups = dot32(rows, place, NT)
    for e in range(blocks):
        dst = send if e % 2 else keep
        dst[e // 2] = ups[:, e * rblk : (e + 1) * rblk].astype(dst.dtype)


def final_kernel(R, rows_each, kept, got, down, up):
    total = kept[0] + got[0].astype(jnp.float32)
    down[...] = total[: 2 * R].T
    up[...] = total[2 * R :, :rows_each]


def solution(mesh):
    C, Dp = mesh.shape["ctx"], mesh.shape["dp"]

    def swap(x, s, axis="ctx"):
        return lax.ppermute(x, axis, [(i, i ^ s) for i in range(mesh.shape[axis])])

    def near(x):
        return pltpu.with_memory_space_constraint(x, pltpu.VMEM)

    def body(queries, keys, teacher, lengths, hidden, adapter, adapter_up):
        tok = queries.shape[1]
        hq = teacher.shape[1]
        S = teacher.shape[2]
        H = hq * C
        DH = queries.shape[2] // H
        KV = keys.shape[2] // DH
        R = adapter.shape[2] // 2
        D = hidden.shape[2]
        q_width = H * DH
        rows_total = adapter_up.shape[0]
        kh = max(1, KV // C)
        W, Wk = hq * DH, kh * DH
        rblk = D // (C * Dp)
        group_cols = (H // KV) * DH
        bf, f32 = jnp.bfloat16, jnp.float32

        def key_col(dst):
            return (dst * W // group_cols) * DH

        def first_plan(me, me_d):
            for s in range(C):
                dst = jnp.bitwise_xor(me, s)
                yield 0, pl.multiple_of(dst * W, 128), s, 0, W
                yield 1, pl.multiple_of(key_col(dst), 128), s, W, Wk
                if s < 2:
                    yield 2, 0, s, W + Wk, 2 * R

        E = C * Dp // 4

        def column(me, me_d, n, e):
            return (jnp.bitwise_xor(me_d, n + e // C * 4) * C + jnp.bitwise_xor(me, e % C)) * rblk

        by_dma = rblk % 128 == 0

        def hidden_plan(me, me_d):
            for n in range(4):
                for e in range(E):
                    yield 0, pl.multiple_of(column(me, me_d, n, e), 128), n, e * rblk, rblk

        def second_plan(me, me_d):
            yield 0, None, 0, None, None
            yield 1, pl.multiple_of(me * W, 128), 1, 0, W
            yield 1, pl.multiple_of(q_width + key_col(me), 128), 2, 0, Wk
            yield 2, None, 3, None, None
            yield 3, None, 4, None, None

        pack, land, slot, rows_each = owner_tables(C, Dp, W, Wk, DH, q_width, group_cols, rows_total, rblk, tok)
        pack, land = jnp.asarray(pack), jnp.asarray(land)
        shapes = [pltpu.VMEM((tok, W + Wk + (2 * R if s < 2 else 0)), bf) for s in range(C)]
        msgs = list(slices(first_plan, 2 * C + 2, (queries[0], keys[0], adapter[0]), shapes))
        for s in range(1, C):
            msgs[s] = swap(msgs[s], s)
        if by_dma:
            hids = list(slices(hidden_plan, 4 * E, (hidden[0],), [pltpu.VMEM((tok, E * rblk), bf)] * 4))
        else:
            blocks, hids = hidden[0].reshape(tok, C * Dp, rblk), []
            me, me_d = lax.axis_index("ctx"), lax.axis_index("dp")
            for n in range(4):
                order = jnp.stack([column(me, me_d, n, e) // rblk for e in range(E)])
                hids.append(jnp.take(blocks, order, axis=1).reshape(tok, E * rblk))
        hids = [hids[0]] + [swap(hids[n], n, "dp") for n in range(1, 4)]
        adapters, bit = jnp.stack([m[:, W + Wk :] for m in msgs[:2]]), 2
        while bit < C:
            adapters = jnp.concatenate([adapters, swap(adapters, bit)])
            bit *= 2
        outs = [
            pltpu.VMEM(teacher.shape[1:], bf),
            pltpu.VMEM((R, W), bf),
            pltpu.VMEM((R, Wk), bf),
            pltpu.VMEM(pack.shape, jnp.int32),
            pltpu.VMEM(land.shape, jnp.int32),
        ]
        teach, up_q, up_k, pack, land = slices(second_plan, 5, (teacher[0], adapter_up.T, pack, land), outs)

        smem = pl.BlockSpec(memory_space=pltpu.SMEM)
        vmem = pl.BlockSpec(memory_space=pltpu.VMEM)
        params = pltpu.CompilerParams(vmem_limit_bytes=24 * 2**20)
        keep, send, dq, dk = pl.pallas_call(
            functools.partial(attend_kernel, C, tok, hq, kh, DH, H, R),
            out_shape=(
                pltpu.VMEM((C // 2, 2 * R, tok), f32),
                pltpu.VMEM((C // 2, 2 * R, tok), f32),
                pltpu.VMEM((S, W), bf),
                pltpu.VMEM((Wk, S), bf),
            ),
            in_specs=[smem] + [vmem] * (C + 3),
            out_specs=tuple([vmem] * 4),
            scratch_shapes=[
                pltpu.VMEM((hq, S, DH), bf),
                pltpu.VMEM((S, Wk), bf),
                pltpu.VMEM((Wk, S), f32),
                pltpu.VMEM((2 * R, S), f32),
            ],
            compiler_params=params,
            name="attend",
        )(lengths, *[near(m) for m in msgs], near(teach), near(up_q), near(up_k))
        low = keep + swap(send, 1)
        bit = 2
        while bit < C:
            both = low.reshape((-1, 2) + low.shape[1:])
            low = both[:, 0] + swap(both[:, 1].astype(bf), bit).astype(f32)
            bit *= 2
        ups, send = pl.pallas_call(
            functools.partial(up_kernel, C, tok, R),
            out_shape=(pltpu.VMEM((2, R, slot), f32), pltpu.VMEM((2, R, slot), bf)),
            in_specs=[vmem] * 4,
            out_specs=(vmem, vmem),
            scratch_shapes=[pltpu.VMEM((S, 2 * R), bf)],
            compiler_params=params,
            name="upgrad",
        )(near(adapters), near(dq), near(dk), near(pack))
        ups = ups + swap(send, 2, "dp").astype(f32)
        low = low.astype(bf)
        lows = [low]
        for n in range(1, 4):
            lows.append(swap(low, n, "dp"))
        got = swap(ups[1].astype(bf), 1, "dp")
        send, keep = pl.pallas_call(
            functools.partial(down_kernel, rblk),
            out_shape=(pltpu.VMEM((E // 2, 2 * R, rblk), bf), pltpu.VMEM((E // 2, 2 * R, rblk), f32)),
            in_specs=[vmem] * 8,
            out_specs=(vmem, vmem),
            compiler_params=params,
            name="down",
        )(*[near(x) for x in (*lows, *hids)])
        up_send, up_keep = pl.pallas_call(
            functools.partial(place_kernel, rblk),
            out_shape=(pltpu.VMEM((E // 2, R, rblk), bf), pltpu.VMEM((E // 2, R, rblk), f32)),
            in_specs=[vmem] * 3,
            out_specs=(vmem, vmem),
            compiler_params=params,
            name="place",
        )(near(ups[0]), near(got), near(land))

        def halves(x):
            both = x.reshape((-1, 2) + x.shape[1:])
            return both[:, 0], both[:, 1].astype(bf)

        rounds = [("ctx", 1 << i) for i in range(C.bit_length() - 1)]
        rounds += [("dp", 4 << i) for i in range(Dp.bit_length() - 3)]
        for axis, bit in rounds[:-1]:
            keep, send = halves(keep + swap(send, bit, axis).astype(f32))
            up_keep, up_send = halves(up_keep + swap(up_send, bit, axis).astype(f32))
        axis, bit = rounds[-1]
        keep = jnp.concatenate([keep, up_keep], axis=1)
        got = swap(jnp.concatenate([send, up_send], axis=1), bit, axis)
        down, up = pl.pallas_call(
            functools.partial(final_kernel, R, rows_each),
            out_shape=(jax.ShapeDtypeStruct((rblk, 2 * R), f32), jax.ShapeDtypeStruct((R, rows_each), f32)),
            in_specs=[vmem, vmem],
            out_specs=(vmem, vmem),
            compiler_params=params,
            name="final",
        )(near(keep), near(got))
        return down, up.T

    placed = (
        P("dp", "ctx", None),
        P("dp", "ctx", None),
        P("dp", "ctx", None, None),
        P("dp"),
        P("dp", "ctx", None),
        P("dp", "ctx", None),
        P(),
    )
    return jax.shard_map(
        body,
        mesh=mesh,
        in_specs=placed,
        out_specs=(P(("dp", "ctx"), None), P(("dp", "ctx"), None)),
        check_vma=False,
    )
```

```python
import functools
import math

import jax
import jax.numpy as jnp
import numpy as np
from jax import lax
from jax.experimental import pallas as pl
from jax.experimental.pallas import tpu as pltpu
from jax.sharding import PartitionSpec as P

NT = (((1,), (1,)), ((), ()))
TN = (((0,), (0,)), ((), ()))


def dot32(a, b, dims=(((1,), (0,)), ((), ()))):
    return lax.dot_general(a, b, dims, preferred_element_type=jnp.float32)


def owner_tables(C, Dp, W, Wk, DH, q_width, group_cols, rows_total, lane_block, lanes):
    rows_each = rows_total // (C * Dp)
    local, groups = [], []
    for c in range(C):
        k_start = q_width + (c * W // group_cols) * DH
        local.append(np.concatenate([c * W + np.arange(W), k_start + np.arange(Wk)]))
        groups.append([np.nonzero(local[c] // rows_each // C % 4 == m)[0] for m in range(4)])
    slot = -(-max(len(g) for four in groups for g in four) // lanes) * lanes
    pack = np.full((C, 4, 4, slot), -1, np.int32)
    land = np.full((C, 4, slot), -1, np.int32)
    for c in range(C):
        for m in range(4):
            rows = local[c][groups[c][m]]
            owner = rows // rows_each
            land[c, m, : len(rows)] = (owner // C // 4 * C + owner % C) * lane_block + rows % rows_each
            for n in range(4):
                pack[c, m, n, : len(groups[c][m ^ n])] = groups[c][m ^ n]
    return pack.reshape(C * 4, 4 * slot), land.reshape(C * 4, slot), slot, rows_each


def slice_kernel(plan, n_in, *refs):
    ins, (*outs, sems) = refs[:n_in], refs[n_in:]
    copies = []
    for n, (i, src, o, dst, width) in enumerate(plan(lax.axis_index("ctx"), lax.axis_index("dp"))):
        source = ins[i] if src is None else ins[i].at[..., pl.ds(src, width)]
        target = outs[o] if dst is None else outs[o].at[..., pl.ds(dst, width)]
        copies.append(pltpu.make_async_copy(source, target, sems.at[n]))
    for c in copies:
        c.start()
    for c in copies:
        c.wait()


def slices(plan, count, ins, out_shapes):
    spec = pl.BlockSpec(memory_space=pltpu.HBM)
    vmem = pl.BlockSpec(memory_space=pltpu.VMEM)
    ins = [pltpu.with_memory_space_constraint(x, pltpu.HBM) for x in ins]
    return pl.pallas_call(
        functools.partial(slice_kernel, plan, len(ins)),
        out_shape=tuple(out_shapes),
        in_specs=[spec] * len(ins),
        out_specs=tuple([vmem] * len(out_shapes)),
        scratch_shapes=[pltpu.SemaphoreType.DMA((count,))],
        compiler_params=pltpu.CompilerParams(vmem_limit_bytes=2**20),
    )(*ins)


def attend_kernel(C, tok, hq, kh, DH, H, R, lengths, *refs):
    msgs = refs[:C]
    teacher, up_q, up_k = refs[C : C + 3]
    keep_out, send_out, dq_buf, dk_out, q_buf, k_buf, dk_buf, low_buf = refs[C + 3 :]
    me, length = lax.axis_index("ctx"), lengths[0]
    W = hq * DH
    per_key = hq // kh
    scale = 1.0 / math.sqrt(DH)
    exp_scale = scale * math.log2(math.e)
    for s in range(C):
        row = pl.multiple_of(jnp.bitwise_xor(me, s) * tok, tok)
        for h in range(hq):
            q_buf[h, pl.ds(row, tok), :] = msgs[s][:, h * DH : (h + 1) * DH]
        k_buf[pl.ds(row, tok), :] = msgs[s][:, W : W + kh * DH]
    dk_buf[...] = jnp.zeros_like(dk_buf)
    row_in = lax.broadcasted_iota(jnp.int32, (tok, 1), 0)
    col_in = lax.broadcasted_iota(jnp.int32, (tok, tok), 1)

    def scores_of(p, g):
        start, ext = p * tok, (p + 1) * tok
        q_all = q_buf[g * per_key : (g + 1) * per_key, start:ext, :].reshape(per_key * tok, DH)
        return q_all, dot32(q_all, k_buf[:ext, g * DH : (g + 1) * DH], NT)

    def grads_of(p, g, scores):
        start, ext = p * tok, (p + 1) * tok
        row_pos = row_in + start
        visible = (col_in + start) <= jnp.minimum(row_pos, length - 1)
        weight = jnp.where(row_pos < length, 1.0 / H, 0.0)
        grads = []
        for n in range(per_key):
            h = g * per_key + n
            sc = scores[n * tok : (n + 1) * tok]
            diag = jnp.where(visible, sc[:, start:], -1e30)
            sc = diag if p == 0 else jnp.concatenate([sc[:, :start], diag], axis=1)
            te_d = jnp.where(visible, teacher[h, start:ext, start:ext].astype(jnp.float32), 0.0)
            te = te_d if p == 0 else jnp.concatenate(
                [teacher[h, start:ext, :start].astype(jnp.float32), te_d], axis=1
            )
            ex = jnp.exp2((sc - jnp.max(sc, axis=1, keepdims=True)) * exp_scale)
            w_s = weight / jnp.sum(ex, axis=1, keepdims=True)
            w_t = weight / jnp.sum(te, axis=1, keepdims=True)
            grads.append((ex * w_s - te * w_t).astype(jnp.bfloat16))
        return grads[0] if per_key == 1 else jnp.concatenate(grads, axis=0)

    def products_of(p, g, q_all, grad):
        start, ext = p * tok, (p + 1) * tok
        dq = (dot32(grad, k_buf[:ext, g * DH : (g + 1) * DH]) * scale).astype(jnp.bfloat16)
        for n in range(per_key):
            h = g * per_key + n
            dq_buf[start:ext, h * DH : (h + 1) * DH] = dq[n * tok : (n + 1) * tok]
        dk_buf[g * DH : (g + 1) * DH, :ext] += dot32(q_all, grad, TN)

    steps = [(p, g) for p in reversed(range(C)) for g in range(kh)]
    lag, ready, done = 1, {}, {}
    for i in range(len(steps) + 2 * lag):
        if i < len(steps):
            ready[i] = scores_of(*steps[i])
        j = i - lag
        if 0 <= j < len(steps):
            q_all, scores = ready.pop(j)
            done[j] = q_all, grads_of(*steps[j], scores)
        j = i - 2 * lag
        if 0 <= j < len(steps):
            products_of(*steps[j], *done.pop(j))
    dq = dq_buf[...]
    dk = (dk_buf[...] * scale).astype(jnp.bfloat16)
    dk_out[...] = dk
    low_buf[:R, :] = dot32(up_q[...], dq, NT)
    low_buf[R:, :] = dot32(up_k[...], dk)
    for s in range(C):
        pos = pl.multiple_of(jnp.bitwise_xor(me, s) * tok, tok)
        (send_out if s % 2 else keep_out)[s // 2] = low_buf[:, pl.ds(pos, tok)]


def up_kernel(C, tok, R, rblk, *refs):
    adapters, dq, dk, pack, land, keep, send, place, a_buf = refs
    me, me_d = lax.axis_index("ctx"), lax.axis_index("dp")
    for s in range(C):
        a_buf[pl.ds(pl.multiple_of(jnp.bitwise_xor(me, s) * tok, tok), tok), :] = adapters[s][...]
    a_q, a_k = a_buf[:, :R], a_buf[:, R:]
    grad_up = jnp.concatenate(
        [dot32(a_q, dq[...], TN).astype(jnp.bfloat16), dot32(a_k.T, dk[...], NT).astype(jnp.bfloat16)], axis=1
    )
    where_to = pack[pl.ds(me * 4 + jnp.bitwise_and(me_d, 3), 1), :]
    pick = lax.broadcasted_iota(jnp.int32, (grad_up.shape[1], where_to.shape[1]), 0) == where_to
    pick = jnp.where(pick, 1.0, 0.0).astype(jnp.bfloat16)
    rows = dot32(grad_up, pick)
    slot = where_to.shape[1] // 4
    for n in range(4):
        dst = send if n // 2 else keep
        dst[n % 2] = rows[:, n * slot : (n + 1) * slot].astype(dst.dtype)
    here = jnp.right_shift(me_d, 2) * lax.axis_size("ctx") + me
    lands = jnp.bitwise_xor(land[pl.ds(me * 4 + jnp.bitwise_and(me_d, 3), 1), :], here * rblk)
    place[...] = jnp.where(lax.broadcasted_iota(jnp.int32, place.shape, 0) == lands, 1.0, 0.0).astype(place.dtype)


def down_kernel(rblk, l0, l1, l2, l3, h0, h1, h2, h3, send, keep):
    acc = None
    for low, hid in zip((l0, l1, l2, l3), (h0, h1, h2, h3)):
        term = dot32(low[0], hid[...])
        acc = term if acc is None else acc + term
    for e in range(h0.shape[1] // rblk):
        dst = send if e % 2 else keep
        dst[e // 2] = acc[:, e * rblk : (e + 1) * rblk].astype(dst.dtype)


def place_kernel(rblk, ups_a, ups_b, place, send, keep):
    rows = (ups_a[...] + ups_b[...].astype(jnp.float32)).astype(jnp.bfloat16)
    ups = dot32(rows, place[...], NT)
    for e in range(2 * keep.shape[0]):
        dst = send if e % 2 else keep
        dst[e // 2] = ups[:, e * rblk : (e + 1) * rblk].astype(dst.dtype)


def final_kernel(R, rows_each, kept, got, down, up):
    total = kept[0] + got[0].astype(jnp.float32)
    down[...] = total[: 2 * R].T
    up[...] = total[2 * R :, :rows_each]


def solution(mesh):
    C, Dp = mesh.shape["ctx"], mesh.shape["dp"]

    def swap(x, s, axis="ctx"):
        return lax.ppermute(x, axis, [(i, i ^ s) for i in range(mesh.shape[axis])])

    def near(x):
        return pltpu.with_memory_space_constraint(x, pltpu.VMEM)

    def body(queries, keys, teacher, lengths, hidden, adapter, adapter_up):
        tok = queries.shape[1]
        hq = teacher.shape[1]
        S = teacher.shape[2]
        H = hq * C
        DH = queries.shape[2] // H
        KV = keys.shape[2] // DH
        R = adapter.shape[2] // 2
        D = hidden.shape[2]
        q_width = H * DH
        rows_total = adapter_up.shape[0]
        kh = max(1, KV // C)
        W, Wk = hq * DH, kh * DH
        rblk = D // (C * Dp)
        group_cols = (H // KV) * DH
        bf, f32 = jnp.bfloat16, jnp.float32

        def key_col(dst):
            return (dst * W // group_cols) * DH

        def first_plan(me, me_d):
            for s in range(C):
                dst = jnp.bitwise_xor(me, s)
                yield 0, pl.multiple_of(dst * W, 128), s, 0, W
                yield 1, pl.multiple_of(key_col(dst), 128), s, W, Wk
                if s < 2:
                    yield 2, 0, s, W + Wk, 2 * R

        E = C * Dp // 4

        def column(me, me_d, n, e):
            return (jnp.bitwise_xor(me_d, n + e // C * 4) * C + jnp.bitwise_xor(me, e % C)) * rblk

        by_dma = rblk % 128 == 0

        def hidden_plan(me, me_d):
            for n in range(4):
                for e in range(E):
                    yield 0, pl.multiple_of(column(me, me_d, n, e), 128), n, e * rblk, rblk

        def second_plan(me, me_d):
            yield 0, None, 0, None, None
            yield 1, pl.multiple_of(me * W, 128), 1, 0, W
            yield 1, pl.multiple_of(q_width + key_col(me), 128), 2, 0, Wk
            yield 2, None, 3, None, None
            yield 3, None, 4, None, None

        pack, land, slot, rows_each = owner_tables(C, Dp, W, Wk, DH, q_width, group_cols, rows_total, rblk, tok)
        pack, land = jnp.asarray(pack), jnp.asarray(land)
        shapes = [pltpu.VMEM((tok, W + Wk + (2 * R if s < 2 else 0)), bf) for s in range(C)]
        msgs = list(slices(first_plan, 2 * C + 2, (queries[0], keys[0], adapter[0]), shapes))
        for s in range(1, C):
            msgs[s] = swap(msgs[s], s)
        if by_dma:
            hids = list(slices(hidden_plan, 4 * E, (hidden[0],), [pltpu.VMEM((tok, E * rblk), bf)] * 4))
        else:
            blocks, hids = hidden[0].reshape(tok, C * Dp, rblk), []
            me, me_d = lax.axis_index("ctx"), lax.axis_index("dp")
            for n in range(4):
                order = jnp.stack([column(me, me_d, n, e) // rblk for e in range(E)])
                hids.append(jnp.take(blocks, order, axis=1).reshape(tok, E * rblk))
        hids = [hids[0]] + [swap(hids[n], n, "dp") for n in range(1, 4)]
        adapters, bit = jnp.stack([m[:, W + Wk :] for m in msgs[:2]]), 2
        while bit < C:
            adapters = jnp.concatenate([adapters, swap(adapters, bit)])
            bit *= 2
        outs = [
            pltpu.VMEM(teacher.shape[1:], bf),
            pltpu.VMEM((R, W), bf),
            pltpu.VMEM((R, Wk), bf),
            pltpu.VMEM(pack.shape, jnp.int32),
            pltpu.VMEM(land.shape, jnp.int32),
        ]
        teach, up_q, up_k, pack, land = slices(second_plan, 5, (teacher[0], adapter_up.T, pack, land), outs)

        smem = pl.BlockSpec(memory_space=pltpu.SMEM)
        vmem = pl.BlockSpec(memory_space=pltpu.VMEM)
        params = pltpu.CompilerParams(vmem_limit_bytes=24 * 2**20)
        keep, send, dq, dk = pl.pallas_call(
            functools.partial(attend_kernel, C, tok, hq, kh, DH, H, R),
            out_shape=(
                pltpu.VMEM((C // 2, 2 * R, tok), f32),
                pltpu.VMEM((C // 2, 2 * R, tok), f32),
                pltpu.VMEM((S, W), bf),
                pltpu.VMEM((Wk, S), bf),
            ),
            in_specs=[smem] + [vmem] * (C + 3),
            out_specs=tuple([vmem] * 4),
            scratch_shapes=[
                pltpu.VMEM((hq, S, DH), bf),
                pltpu.VMEM((S, Wk), bf),
                pltpu.VMEM((Wk, S), f32),
                pltpu.VMEM((2 * R, S), f32),
            ],
            compiler_params=params,
            name="attend",
        )(lengths, *[near(m) for m in msgs], near(teach), near(up_q), near(up_k))
        low = keep + swap(send, 1)
        bit = 2
        while bit < C:
            both = low.reshape((-1, 2) + low.shape[1:])
            low = both[:, 0] + swap(both[:, 1].astype(bf), bit).astype(f32)
            bit *= 2
        ups, send, place = pl.pallas_call(
            functools.partial(up_kernel, C, tok, R, rblk),
            out_shape=(pltpu.VMEM((2, R, slot), f32), pltpu.VMEM((2, R, slot), bf), pltpu.VMEM((E * rblk, slot), bf)),
            in_specs=[vmem] * 5,
            out_specs=(vmem, vmem, vmem),
            scratch_shapes=[pltpu.VMEM((S, 2 * R), bf)],
            compiler_params=params,
            name="upgrad",
        )(near(adapters), near(dq), near(dk), near(pack), near(land))
        ups = ups + swap(send, 2, "dp").astype(f32)
        low = low.astype(bf)
        lows = [low]
        for n in range(1, 4):
            lows.append(swap(low, n, "dp"))
        got = swap(ups[1].astype(bf), 1, "dp")
        send, keep = pl.pallas_call(
            functools.partial(down_kernel, rblk),
            out_shape=(pltpu.VMEM((E // 2, 2 * R, rblk), bf), pltpu.VMEM((E // 2, 2 * R, rblk), f32)),
            in_specs=[vmem] * 8,
            out_specs=(vmem, vmem),
            compiler_params=params,
            name="down",
        )(*[near(x) for x in (*lows, *hids)])
        up_send, up_keep = pl.pallas_call(
            functools.partial(place_kernel, rblk),
            out_shape=(pltpu.VMEM((E // 2, R, rblk), bf), pltpu.VMEM((E // 2, R, rblk), f32)),
            in_specs=[vmem] * 3,
            out_specs=(vmem, vmem),
            compiler_params=params,
            name="place",
        )(near(ups[0]), near(got), near(place))

        def halves(x):
            both = x.reshape((-1, 2) + x.shape[1:])
            return both[:, 0], both[:, 1].astype(bf)

        rounds = [("ctx", 1 << i) for i in range(C.bit_length() - 1)]
        rounds += [("dp", 4 << i) for i in range(Dp.bit_length() - 3)]
        for axis, bit in rounds[:-1]:
            keep, send = halves(keep + swap(send, bit, axis).astype(f32))
            up_keep, up_send = halves(up_keep + swap(up_send, bit, axis).astype(f32))
        axis, bit = rounds[-1]
        keep = jnp.concatenate([keep, up_keep], axis=1)
        got = swap(jnp.concatenate([send, up_send], axis=1), bit, axis)
        down, up = pl.pallas_call(
            functools.partial(final_kernel, R, rows_each),
            out_shape=(jax.ShapeDtypeStruct((rblk, 2 * R), f32), jax.ShapeDtypeStruct((R, rows_each), f32)),
            in_specs=[vmem, vmem],
            out_specs=(vmem, vmem),
            compiler_params=params,
            name="final",
        )(near(keep), near(got))
        return down, up.T

    placed = (
        P("dp", "ctx", None),
        P("dp", "ctx", None),
        P("dp", "ctx", None, None),
        P("dp"),
        P("dp", "ctx", None),
        P("dp", "ctx", None),
        P(),
    )
    return jax.shard_map(
        body,
        mesh=mesh,
        in_specs=placed,
        out_specs=(P(("dp", "ctx"), None), P(("dp", "ctx"), None)),
        check_vma=False,
    )
```
